128 devices in a mesh: dom: 32 (over z, x, core), bin: 4 (over y).
Axes of the slice: x: 4, y: 4, z: 4, core: 2. Of those that a mesh axis runs over, the one named last changes fastest.
Arguments:
- displacement: float32 [3, 256, 64, 512], P(None, 'dom', 'bin'), may hold values from -0.3 to 0.3
- velocity: float32 [3, 256, 64, 512], P(None, 'dom', 'bin'), may hold values from -0.3 to 0.3
- moduli: float32 [2, 256, 64, 512], P(None, 'dom', 'bin'), may hold values from 0.2 to 2
- nodal_mass: float32 [256, 64, 512], P('dom', 'bin'), may hold values from 0.5 to 2
- segment_node: int32 [131072], P(('dom', 'bin')), may hold values from 0 to 65535
- segment_base: float32 [3, 131072], P(None, ('dom', 'bin')), may hold values from 0 to 1
- contact_bin: int32 [4, 1024, 1], P(None, ('dom', 'bin')), may hold values from 0 to 3; in each aligned block of 8 rows (0 to 7, 8 to 15, ..., all dimensions but the last counted through in order) at most 4 rows name the same one
- element_tile: int32 [256, 64, 512], P('dom', 'bin'), may hold values from 0 to 32767, as said below
Outputs:
- new_displacement: float32 [3, 256, 64, 512], P(None, 'dom', 'bin')
- new_velocity: float32 [3, 256, 64, 512], P(None, 'dom', 'bin')
- tile_heat: float32 [32768], P(('dom', 'bin'))
The draws below stay inside these ranges and needn't reach their ends.
Inputs may be any that keep to these rules, and one draw needn't show every extreme that they name: `contact_bin`: in each substep no device sends more than 4 of its blocks to one bin, and at least one device sends exactly 4. `segment_node`: A node of the holding device's own block, numbered row-major over (8, 16, 512). `element_tile`: tiles are numbered device-major (256 to a device, devices in the order dom, then bin). An element's tile belongs to the device that holds it, except that elements of a device's first or last layer along the first dimension may take a tile of the device one step lower or higher along dom (same bin index).
All inputs are finite; a program needn't handle non-finite values.
Results may differ from the reference program's by a relative error of at most 0.0003.
Values sent between devices are 32-bit elements; how exact they have to be, the bound alone decides.
A program may use at most 128 MiB of HBM per device.

```python
import math
import jax
import jax.numpy as jnp
import numpy as np
from jax import lax

CX = 8
CY = 16
NZ = 512
SUB = 4
SEG = 128
BLK_DEV = 8
TILE_DEV = 256
CAP = 4
NX = 256
NY = 64
BLOCKS = 1024
SEGS = 131072
TILES = 32768
N_DOM = 32
N_BIN = 4


def draw_element_tile(key, part):
    pos_x = jnp.arange(NX, dtype=jnp.int32)[:, None, None]
    pos_y = jnp.arange(NY, dtype=jnp.int32)[None, :, None]
    pos_z = jnp.arange(NZ, dtype=jnp.int32)[None, None, :]
    dom_index = pos_x // CX
    bin_index = pos_y // CY
    local_x = pos_x % CX
    local_y = pos_y % CY
    local_order = (local_x * CY + local_y) * NZ + pos_z
    local_tile = local_order * TILE_DEV // (CX * CY * NZ)
    moving = jax.random.randint(jax.random.fold_in(key, 11), (NX, NY, NZ), 0, 2)
    down = jnp.logical_and(local_x == 0, dom_index > 0).astype(jnp.int32) * moving
    up = jnp.logical_and(local_x == CX - 1, dom_index < N_DOM - 1).astype(jnp.int32) * moving
    target_dom = dom_index - down + up
    device = target_dom * N_BIN + bin_index
    return (device * TILE_DEV + local_tile).astype(jnp.int32)


def place_ends(values, own_key, low, largest):
    index_at = [jax.random.randint(jax.random.fold_in(own_key, axis), (), 0, length) for axis, length in enumerate(values.shape)]
    longest = values.shape.index(max(values.shape))
    beside = index_at[:longest] + [(index_at[longest] + 1) % values.shape[longest]] + index_at[longest + 1:]
    return values.at[tuple(index_at)].set(low).at[tuple(beside)].set(largest)


def block_scale(rng, dims, cuts, low, top_value):
    def one(dim, parts):
        steps = jax.random.uniform(jax.random.fold_in(jax.random.fold_in(rng, 6), dim), (parts,), jnp.float32, low / len(cuts), top_value / len(cuts))
        return jnp.repeat(jnp.exp(steps), dims[dim] // parts).reshape((-1,) + (1,) * (len(dims) - dim - 1))

    factor_of = one(*cuts[0])
    for cut in cuts[1:]:
        factor_of = factor_of * one(*cut)
    return factor_of


def assign_block(own_key, own, number, rows, number_of, top, most, slope):
    order = jax.random.permutation(own_key, number_of)
    crowded, ordinary = load_shares(number_of, rows * top, most, slope, True), load_shares(number_of, rows * top, most, slope, False)
    places = jnp.arange(number_of)

    def named(lengths, rotation):
        used = int((lengths > 0).sum())
        fixed = max(1, used // 4)
        moved = fixed + (places - fixed + rotation * (used - fixed)) % max(1, number_of - fixed)
        return jnp.zeros((number_of,), jnp.int32).at[order[jnp.where(places < fixed, places, moved)]].set(jnp.asarray(lengths, jnp.int32))

    lengths = jnp.where(number % 4 == 0, named(crowded, number // 4), named(ordinary, number - number // 4 - 1))
    mixed = jax.random.permutation(jax.random.fold_in(own, 3), number_of)
    donor, taker = mixed[0:number_of // 2 * 2:2], mixed[1:number_of // 2 * 2:2]
    slack = jnp.minimum(lengths[donor] - 1, most - lengths[taker]) // 2
    slack = jnp.where((donor == order[0]) | (taker == order[0]) | (lengths[taker] == 0), 0, jnp.maximum(slack, 0))
    moved = jax.random.randint(jax.random.fold_in(own, 4), (number_of // 2,), 0, 1 << 20) % (slack + 1)
    lengths = lengths.at[donor].add(-moved).at[taker].add(moved)
    items = jnp.searchsorted(jnp.cumsum(lengths), jnp.arange(rows * top), side="right").astype(jnp.int32)
    grid = items.reshape(top, rows).T
    grid = grid[jax.random.permutation(jax.random.fold_in(own, 1), rows)]
    rotation = jax.random.randint(jax.random.fold_in(own, 2), (rows, 1), 0, top)
    return jnp.take_along_axis(grid, (jnp.arange(top)[None, :] + rotation) % top, axis=1)


def load_shares(count, total, most, slope, full):
    portions = [(1 << 20) // math.isqrt(rank ** slope) + 1 for rank in range(1, count + 1)]
    largest = most if full else min(most, max(-(-total // count), total * portions[0] // sum(portions)))
    least = 1 if total - largest >= count - 1 else 0
    counts, spare = [largest] + [least] * (count - 1), total - largest - least * (count - 1)
    while spare > 0:
        candidates = [i for i in range(1, count) if counts[i] < largest] or [i for i in range(1, count) if counts[i] < most]
        whole, remaining = sum([portions[i] for i in candidates]), spare
        for i in candidates:
            addition = min(most - counts[i], max(1, remaining * portions[i] // whole), spare)
            counts[i] = counts[i] + addition
            spare = spare - addition
    return np.array(counts)


def noise(rng, shape, width, limit, shards=(), held_as=jnp.bfloat16):
    result = jax.random.normal(rng, shape, jnp.float32) * width
    if len(shards) > 0:
        result = block_scale(rng, shape, shards, -0.22, 0.18) * result
    return jnp.clip(result, min=-limit, max=limit).astype(held_as)


def setup_inputs(seed: int = 0) -> dict:
    arg_keys = jax.random.split(jax.random.key(seed), 9)
    displacement = noise(arg_keys[0], (3, NX, NY, NZ), 0.05, 0.3, ((1, 32), (2, 4)), jnp.float32)
    velocity = noise(arg_keys[1], (3, NX, NY, NZ), 0.05, 0.3, ((1, 32), (2, 4)), jnp.float32)
    moduli = jnp.clip(jnp.exp(math.log(2.0) - 2.3025851 * jax.random.uniform(arg_keys[2], (2, NX, NY, NZ), jnp.float32) ** block_scale(arg_keys[2], (2, NX, NY, NZ), ((1, 32), (2, 4)), -0.2, 0.2)), 0.2, 2.0)
    nodal_mass = jnp.clip(jnp.exp(math.log(2.0) - 1.3862944 * jax.random.uniform(arg_keys[3], (NX, NY, NZ), jnp.float32) ** block_scale(arg_keys[3], (NX, NY, NZ), ((0, 32), (1, 4)), -0.2, 0.2)), 0.5, 2.0)
    segment_node = place_ends(jax.random.randint(arg_keys[4], (SEGS,), 0, CX * CY * NZ), jax.random.fold_in(arg_keys[4], 1), 0, (CX * CY * NZ) - 1).astype(jnp.int32)
    segment_base = jnp.clip(1.0 * jax.random.uniform(arg_keys[5], (3, SEGS), jnp.float32) ** block_scale(arg_keys[5], (3, SEGS), ((1, 128),), -0.2, 0.2), 0.0, 1.0)
    contact_bin_keys = jax.random.split(jax.random.fold_in(arg_keys[6], 1), SUB * BLOCKS // BLK_DEV)
    contact_bin_turns = jax.random.permutation(jax.random.fold_in(arg_keys[6], 3), SUB * BLOCKS // BLK_DEV)
    contact_bin = jax.vmap(lambda own, number: assign_block(jax.random.fold_in(arg_keys[6], 2), own, number, BLK_DEV, N_BIN, 1, CAP, 2))(contact_bin_keys, contact_bin_turns).reshape((SUB, BLOCKS, 1))
    element_tile = draw_element_tile(jax.random.fold_in(arg_keys[8], 71), 0)
    return {"displacement": displacement, "velocity": velocity, "moduli": moduli, "nodal_mass": nodal_mass, "segment_node": segment_node, "segment_base": segment_base, "contact_bin": contact_bin, "element_tile": element_tile}


RADIUS = 0.09
PENALTY = 4.0
SHORT_GAIN = 100.0
TIME_STEP = 0.2
CORNERS = ((0, 0, 0), (0, 0, 1), (0, 1, 0), (0, 1, 1), (1, 0, 0), (1, 0, 1), (1, 1, 0), (1, 1, 1))

def corner_forces(padded, moduli_used, extent_x, extent_y):
    pieces = []
    for a, b, c in CORNERS:
        piece = padded[:, a:a + extent_x, b:b + extent_y]
        if c == 1:
            piece = jnp.roll(piece, -1, axis=3)
        pieces.append(piece)
    corner_signs = [[2 * bit - 1 for bit in corner] for corner in CORNERS]
    gradient = [[0.25 * sum((corner_signs[k][q] * pieces[k][p] for k in range(8))) for q in range(3)] for p in range(3)]
    volume_strain = gradient[0][0] + gradient[1][1] + gradient[2][2]
    stress = [[moduli_used[1] * (gradient[p][q] + gradient[q][p]) + (moduli_used[0] * volume_strain if p == q else 0.0) for q in range(3)] for p in range(3)]
    corner_list = []
    for k in range(8):
        corner_list.append(jnp.stack([-0.25 * sum((corner_signs[k][q] * stress[p][q] for q in range(3))) for p in range(3)]))
    return corner_list

def spread_corners(corner_list):
    nodal = 0.0
    for k in range(8):
        a, b, c = CORNERS[k]
        moved = jnp.roll(corner_list[k], c, axis=3)
        nodal = nodal + jnp.pad(moved, ((0, 0), (a, 1 - a), (b, 1 - b), (0, 0)))
    return nodal

def contact_terms(segment_pool, alive_mask):
    row_blocks = segment_pool.reshape(3, -1, SEG).transpose(1, 0, 2)

    def one_block(target):
        offsets = target[:, :, None] - segment_pool[:, None, :]
        distance = jnp.sqrt(lax.optimization_barrier(jnp.sum(offsets * offsets, axis=0)))
        pressure = jnp.maximum(RADIUS - distance, 0.0) * alive_mask[None, :]
        pushing = PENALTY * lax.optimization_barrier(jnp.sum(offsets * (pressure / jnp.maximum(distance, 0.25 * RADIUS))[None], axis=2))
        heating = SHORT_GAIN * lax.optimization_barrier(jnp.sum(pressure * pressure, axis=1))
        return (pushing, heating)
    return lax.map(one_block, row_blocks)

def reference(displacement, velocity, moduli, nodal_mass, segment_node, segment_base, contact_bin, element_tile):
    devices = N_DOM * N_BIN
    owner = jnp.arange(SEGS, dtype=jnp.int32) // (BLK_DEV * SEG)
    grid_x = owner // N_BIN * CX + segment_node // (CY * NZ)
    grid_y = owner % N_BIN * CY + segment_node // NZ % CY
    grid_z = segment_node % NZ
    segment_tile = element_tile[grid_x, grid_y, grid_z]
    block_owner = jnp.arange(BLOCKS, dtype=jnp.int32) // BLK_DEV
    source = block_owner % N_BIN
    tile_heat = jnp.zeros((TILES,), jnp.float32)
    for step in range(SUB):
        points = segment_base + displacement[:, grid_x, grid_y, grid_z]
        target_bin = contact_bin[step, :, 0]
        onehot = (target_bin.reshape(devices, BLK_DEV)[:, :, None] == jnp.arange(N_BIN, dtype=jnp.int32)[None, None, :]).astype(jnp.int32)
        slot_rank = jnp.cumsum(onehot, axis=1) - onehot
        slot_index = lax.optimization_barrier(jnp.sum(slot_rank * onehot, axis=2)).reshape(BLOCKS)
        group = block_owner // N_BIN * N_BIN + target_bin
        blocks = points.reshape(3, BLOCKS, SEG).transpose(1, 0, 2)
        buffers = jnp.zeros((devices, N_BIN, CAP, 3, SEG), jnp.float32).at[group, source, slot_index].set(blocks)
        alive = jnp.zeros((devices, N_BIN, CAP), jnp.float32).at[group, source, slot_index].set(1.0)

        def per_group(pair):
            group_buffer, group_alive = pair
            segment_pool = group_buffer.transpose(2, 0, 1, 3).reshape(3, -1)
            alive_mask = jnp.repeat(group_alive.reshape(-1), SEG)
            pushing, heating = contact_terms(segment_pool, alive_mask)
            return (pushing.reshape(N_BIN, CAP, 3, SEG), heating.reshape(N_BIN, CAP, SEG))
        push_all, heat_all = lax.map(per_group, (buffers, alive))
        segment_push = push_all[group, source, slot_index].transpose(1, 0, 2).reshape(3, SEGS)
        segment_heat = heat_all[group, source, slot_index].reshape(SEGS)
        tile_heat = tile_heat + jax.ops.segment_sum(segment_heat, segment_tile, num_segments=TILES)
        contact = jnp.zeros((3, NX, NY, NZ), jnp.float32).at[:, grid_x, grid_y, grid_z].add(segment_push)
        padded = jnp.pad(displacement, ((0, 0), (0, 1), (0, 1), (0, 0)))
        internal = spread_corners(corner_forces(padded, moduli, NX, NY))[:, :NX, :NY]
        velocity = velocity + TIME_STEP * (internal + contact) / nodal_mass[None]
        displacement = displacement + TIME_STEP * velocity
    return (displacement, velocity, tile_heat)
```

```python
import functools

import jax
import jax.numpy as jnp
from jax import lax
from jax.experimental import pallas as pl
from jax.experimental.pallas import tpu as pltpu
from jax.sharding import PartitionSpec as P

SUB = 4
SEG = 128
TILE_DEV = 256
RADIUS = 0.09
PENALTY = 4.0
SHORT_GAIN = 100.0
TIME_STEP = 0.2

CX, CY, ZT = 8, 16, 4
NBLK, CAP, NBIN = 8, 4, 4
NSEG = NBLK * SEG
ROWS = CX * ZT * CY
PIECES = 3
FAR = 1e12
MESH = pl.DeviceIdType.MESH
F32, BF16, I32 = jnp.float32, jnp.bfloat16, jnp.int32


def pieces_of(value):
    parts = []
    for _ in range(PIECES):
        part = value.astype(BF16)
        parts.append(part)
        value = value - part.astype(F32)
    return parts


def lanes_of(shape):
    return lax.broadcasted_iota(I32, shape, len(shape) - 1)


def next_z(value):
    turned = pltpu.roll(value, 127, 2)
    beyond = jnp.concatenate([turned[1:], turned[:1]], axis=0)
    return jnp.where(lanes_of(value.shape) == 127, beyond, turned)


def last_z(value):
    turned = pltpu.roll(value, 1, 2)
    before = jnp.concatenate([turned[-1:], turned[:-1]], axis=0)
    return jnp.where(lanes_of(value.shape) == 0, before, turned)


def spread_row(row):
    return jnp.broadcast_to(row, (SEG, SEG)).T


def kernel(
    disp_in, velo_in, moduli_in, mass_in, tile_in, node_ref, base_ref, bins_ref,
    disp_out, velo_out, heat_out,
    disp, velo, moduli, inverse, tiles,
    one_seg, one_node, lane_col, base_col, tile_lane, tile_row,
    split_disp, split_push, seg_col, seg_row, outgoing, pool, spread,
    push_acc, heat_acc, contact,
    grads, stress, near, far,
    col_out, col_in, corner_out, corner_in,
    layer_force_out, layer_force_in, col_force_out, col_force_in,
    corner_force_out, corner_force_in,
    heat_parts, heat_in, slots,
    in_sem, out_sem, send_sem, recv_sem, point_send, point_recv, heat_send, heat_recv,
):
    dom, own = lax.axis_index("dom"), lax.axis_index("bin")
    doms, bins = lax.axis_size("dom"), lax.axis_size("bin")
    dom_up, dom_low = dom < doms - 1, dom > 0
    bin_up, bin_low = own < bins - 1, own > 0
    diag_up, diag_low = jnp.logical_and(dom_up, bin_up), jnp.logical_and(dom_low, bin_low)

    loads = []
    for z in range(ZT):
        z_at = pl.ds(z * 128, 128)
        loads.append((disp_in.at[:, :, :, z_at], disp.at[:, pl.ds(0, CX), z, pl.ds(8, CY), :]))
        loads.append((tile_in.at[:, :, z_at], tiles.at[:, z]))
        loads.append((moduli_in.at[:, :, :, z_at], moduli.at[:, :, z]))
        loads.append((mass_in.at[:, :, z_at], inverse.at[:, z]))
        loads.append((velo_in.at[:, :, :, z_at], velo.at[:, :, z]))
    loads = [pltpu.make_async_copy(a, b, in_sem.at[i]) for i, (a, b) in enumerate(loads)]
    for load in loads:
        load.start()

    disp[:, CX, :, :, :] = jnp.zeros((3, ZT, 32, 128), F32)
    col_in[...] = jnp.zeros_like(col_in)
    corner_in[...] = jnp.zeros_like(corner_in)
    layer_force_in[...] = jnp.zeros_like(layer_force_in)
    col_force_in[...] = jnp.zeros_like(col_force_in)
    corner_force_in[...] = jnp.zeros_like(corner_force_in)
    heat_in[...] = jnp.zeros_like(heat_in)
    for k in range(6):
        stress[k, 0] = jnp.zeros((ZT, CY, 128), F32)
        stress[k, CX + 1] = jnp.zeros((ZT, CY, 128), F32)
    for p in range(3):
        far[p, CX, :, 0:8, :] = jnp.zeros((ZT, 8, 128), F32)
        seg_row[NBLK] = jnp.full((4, 128), FAR, F32)

    barrier = pltpu.get_barrier_semaphore()
    peers = [(dom, lax.rem(own + i, bins), None) for i in range(1, NBIN)]
    peers += [(dom + 1, own, dom_up), (dom - 1, own, dom_low)]
    peers += [(dom + 1, own + 1, diag_up), (dom - 1, own - 1, diag_low)]
    for to_dom, to_bin, exists in peers:
        def greet(to_dom=to_dom, to_bin=to_bin):
            pl.semaphore_signal(barrier, inc=1, device_id=(to_dom, to_bin), device_id_type=MESH)
        if exists is None:
            greet()
        else:
            pl.when(exists)(greet)

    def fill_slots(step, carry):
        named = [bins_ref[step * NBLK + b] for b in range(NBLK)]
        for k in range(NBIN):
            count = jnp.int32(0)
            found = [jnp.int32(NBLK)] * CAP
            for b in range(NBLK):
                same = named[b] == k
                for rank in range(CAP):
                    found[rank] = jnp.where(
                        jnp.logical_and(same, count == rank), jnp.int32(b), found[rank]
                    )
                count = count + same.astype(I32)
            for rank in range(CAP):
                slots[(step * NBIN + k) * CAP + rank] = found[rank]
        return carry

    lax.fori_loop(0, SUB, fill_slots, 0)

    eye = lax.broadcasted_iota(I32, (SEG, SEG), 0) == lanes_of((SEG, SEG))

    def place_block(b, carry):
        node = node_ref[pl.ds(b, 1), :]
        x, y = lax.shift_right_logical(node, 13), lax.shift_right_logical(node, 9) & 15
        z = lax.shift_right_logical(node, 7) & 3
        row = (x * ZT + z) * CY + y
        lane = node & 127
        at = pl.ds(pl.multiple_of(b * SEG, SEG), SEG)
        row_ids = lax.broadcasted_iota(I32, (ROWS, SEG), 0)
        hits = jnp.where(row_ids == row, 1.0, 0.0).astype(BF16)
        for p in range(PIECES):
            p_at = pl.ds(pl.multiple_of(p * NSEG + b * SEG, SEG), SEG)
            one_seg[:, p_at] = hits
        row_col = spread_row(row.astype(F32))
        ids = lanes_of((SEG, SEG)).astype(F32)
        for part in range(ROWS // 128):
            hits = jnp.where(row_col == ids + float(128 * part), 1.0, 0.0).astype(BF16)
            for p in range(PIECES):
                one_node[at, p * ROWS + part * 128 : p * ROWS + part * 128 + 128] = hits
        lane_col[at, :] = spread_row(lane.astype(F32))
        for c in range(3):
            base_col[c, at, :] = spread_row(base_ref[c, pl.ds(b, 1), :])
        heat_acc[at, :] = jnp.zeros((SEG, SEG), F32)
        return carry

    lax.fori_loop(0, NBLK, place_block, 0)

    for load in loads:
        load.wait()

    def scale(x, carry):
        for k in range(2):
            moduli[k, x] = moduli[k, x] * -0.0625
        inverse[x] = TIME_STEP / inverse[x]
        return carry

    lax.fori_loop(0, CX, scale, 0)

    greeted = jnp.int32(NBIN - 1)
    for _, _, exists in peers[NBIN - 1 :]:
        greeted = greeted + exists.astype(I32)
    pl.semaphore_wait(barrier, greeted)

    def remote(src, dst, index, to_dom, to_bin):
        return pltpu.make_async_remote_copy(
            src_ref=src, dst_ref=dst, send_sem=send_sem.at[index], recv_sem=recv_sem.at[index],
            device_id=(to_dom, to_bin), device_id_type=MESH,
        )

    inner = pl.ds(8, CY)
    layer_copy = remote(disp.at[:, 0, :, inner, :], disp.at[:, CX, :, inner, :], 0, dom - 1, own)
    col_copy = remote(col_out, col_in, 1, dom, own - 1)
    corner_copy = remote(corner_out, corner_in, 2, dom - 1, own - 1)
    layer_force_copy = remote(layer_force_out, layer_force_in, 3, dom + 1, own)
    col_force_copy = remote(col_force_out, col_force_in, 4, dom, own + 1)
    corner_force_copy = remote(corner_force_out, corner_force_in, 5, dom + 1, own + 1)

    def touching(ahead, step, fresh):
        def rows_of(i, carry):
            at = pl.ds(pl.multiple_of(i * 16, 16), 16)
            mine = [seg_col[c, at, :].reshape(2, 8, 128) for c in range(3)]
            named = bins_ref[step * NBLK + i // 8]
            sums = [
                jnp.zeros((2, 8, 128), F32) if fresh else push_acc[c, at, :].reshape(2, 8, 128)
                for c in range(3)
            ]
            heat = heat_acc[at, :].reshape(2, 8, 128)
            for i in ahead:
                for k in range(CAP):
                    slot = i * (NBIN * CAP) + named * CAP + k
                    delta = [mine[c] - spread[slot, c] for c in range(3)]
                    square = delta[0] * delta[0] + delta[1] * delta[1] + delta[2] * delta[2]
                    square = jnp.maximum(square, 1e-30)
                    over = lax.rsqrt(square)
                    pressure = jnp.maximum(RADIUS - square * over, 0.0)
                    weight = pressure * jnp.minimum(over, 1.0 / (0.25 * RADIUS))
                    heat = heat + pressure * pressure
                    sums = [sums[c] + weight * delta[c] for c in range(3)]
            for c in range(3):
                push_acc[c, at, :] = sums[c].reshape(16, 128)
            heat_acc[at, :] = heat.reshape(16, 128)
            return carry

        lax.fori_loop(0, NSEG // 16, rows_of, 0)

    def substep(step, carry):
        parity = lax.rem(step, 2)

        for c in range(3):
            for z in range(ZT):
                corner_out[c * ZT + z : c * ZT + z + 1, :] = disp[c, 0, z, 8:9, :]
                for x in range(CX):
                    col_out[c, z, x : x + 1, :] = disp[c, x, z, 8:9, :]
        pl.when(dom_low)(layer_copy.start)
        pl.when(bin_low)(col_copy.start)
        pl.when(diag_low)(corner_copy.start)

        def split(x, carry):
            for c in range(3):
                value = disp[c, x, :, 8 : 8 + CY, :].reshape(ZT * CY, 128)
                for p, part in enumerate(pieces_of(value)):
                    at = pl.ds(pl.multiple_of(p * ROWS + x * (ZT * CY), ZT * CY), ZT * CY)
                    split_disp[at, c * 128 : c * 128 + 128] = part
            return carry

        lax.fori_loop(0, CX, split, 0)

        def positions(b, carry):
            at = pl.ds(pl.multiple_of(b * SEG, SEG), SEG)
            picked = jnp.dot(one_node[at, :], split_disp[...], preferred_element_type=F32)
            mask = lane_col[at, :] == lanes_of((SEG, SEG)).astype(F32)
            for c in range(3):
                moved = jnp.where(mask, picked[:, c * 128 : c * 128 + 128], 0.0)
                column = base_col[c, at, :] + jnp.sum(moved, axis=1, keepdims=True)
                seg_col[c, at, :] = column
                seg_row[b, c : c + 1, :] = jnp.sum(
                    jnp.where(eye, column, 0.0), axis=0, keepdims=True
                )
            return carry

        lax.fori_loop(0, NBLK, positions, 0)
        for slot in range(NBIN * CAP):
            block = seg_row[slots[step * (NBIN * CAP) + slot]]
            outgoing[slot] = block
            for c in range(3):
                spread[slot, c] = jnp.broadcast_to(block[c : c + 1, :], (8, 128))
        for i in range(1, NBIN):
            point_copy(i, parity).start()

        touching([0], step, True)

        pl.when(dom_up)(layer_copy.wait_recv)
        pl.when(bin_up)(col_copy.wait_recv)
        pl.when(diag_up)(corner_copy.wait_recv)
        for c in range(3):
            for z in range(ZT):
                disp[c, CX, z, 24:25, :] = corner_in[c * ZT + z : c * ZT + z + 1, :]
                for x in range(CX):
                    disp[c, x, z, 24:25, :] = col_in[c, z, x : x + 1, :]

        def corners(x, carry):
            for c in range(3):
                low, high = disp[c, x, :, 8:24, :], disp[c, x, :, 9:25, :]
                total, gap = low + high, high - low
                total_next, gap_next = next_z(total), next_z(gap)
                grads[c, 0, x] = total + total_next
                grads[c, 1, x] = gap + gap_next
                grads[c, 2, x] = total_next - total
            return carry

        lax.fori_loop(0, CX + 1, corners, 0)

        def stresses(x, carry):
            g = [
                [grads[c, 0, x + 1] - grads[c, 0, x]]
                + [grads[c, q, x] + grads[c, q, x + 1] for q in (1, 2)]
                for c in range(3)
            ]
            lame, shear = moduli[0, x], moduli[1, x]
            volume = lame * (g[0][0] + g[1][1] + g[2][2])
            for p in range(3):
                stress[p, x + 1] = shear * (g[p][p] + g[p][p]) + volume
            stress[3, x + 1] = shear * (g[0][1] + g[1][0])
            stress[4, x + 1] = shear * (g[0][2] + g[2][0])
            stress[5, x + 1] = shear * (g[1][2] + g[2][1])
            return carry

        lax.fori_loop(0, CX, stresses, 0)

        def forces(x, carry):
            for p, (kx, ky, kz) in enumerate(((0, 3, 4), (3, 1, 5), (4, 5, 2))):
                along_x = stress[kx, x] - stress[kx, x + 1]
                along_y = stress[ky, x] + stress[ky, x + 1]
                along_z = stress[kz, x] + stress[kz, x + 1]
                minus, plus = along_x - along_y, along_x + along_y
                near[p, x] = (minus - along_z) + last_z(minus + along_z)
                far[p, x, :, 8:24, :] = (plus - along_z) + last_z(plus + along_z)
            return carry

        lax.fori_loop(0, CX + 1, forces, 0)
        for p in range(3):
            layer_force_out[p] = near[p, CX] + far[p, CX, :, 7:23, :]
            for z in range(ZT):
                corner_force_out[p * ZT + z : p * ZT + z + 1, :] = far[p, CX, z, 23:24, :]
                for x in range(CX):
                    col_force_out[p, z, x : x + 1, :] = far[p, x, z, 23:24, :]
        pl.when(dom_up)(layer_force_copy.start)
        pl.when(bin_up)(col_force_copy.start)
        pl.when(diag_up)(corner_force_copy.start)

        for i in range(1, NBIN):
            point_copy(i, parity).wait_recv()

        def spread_slot(slot, carry):
            for i in range(1, NBIN):
                block = pool[parity, lax.rem(own + i, bins), slot]
                for c in range(3):
                    spread[i * (NBIN * CAP) + slot, c] = jnp.broadcast_to(
                        block[c : c + 1, :], (8, 128)
                    )
            return carry

        lax.fori_loop(0, NBIN * CAP, spread_slot, 0)
        touching(range(1, NBIN), step, False)

        def lay_push(b, carry):
            at = pl.ds(pl.multiple_of(b * SEG, SEG), SEG)
            mask = lane_col[at, :] == lanes_of((SEG, SEG)).astype(F32)
            for c in range(3):
                total = jnp.sum(push_acc[c, at, :], axis=1, keepdims=True)
                laid = jnp.where(mask, PENALTY * total, 0.0)
                for p, part in enumerate(pieces_of(laid)):
                    p_at = pl.ds(pl.multiple_of(p * NSEG + b * SEG, SEG), SEG)
                    split_push[p_at, c * 128 : c * 128 + 128] = part
            return carry

        lax.fori_loop(0, NBLK, lay_push, 0)
        pushed = jnp.dot(one_seg[...], split_push[...], preferred_element_type=F32)
        for c in range(3):
            contact[c] = pushed[:, c * 128 : c * 128 + 128]

        pl.when(dom_low)(layer_force_copy.wait_recv)
        pl.when(bin_low)(col_force_copy.wait_recv)
        pl.when(diag_low)(corner_force_copy.wait_recv)
        for p in range(3):
            near[p, 0] = near[p, 0] + layer_force_in[p]
            for z in range(ZT):
                near[p, 0, z, 0:1, :] = (
                    near[p, 0, z, 0:1, :] + corner_force_in[p * ZT + z : p * ZT + z + 1, :]
                )
                for x in range(CX):
                    far[p, x, z, 7:8, :] = col_force_in[p, z, x : x + 1, :]
        pl.when(dom_low)(layer_copy.wait_send)
        pl.when(bin_low)(col_copy.wait_send)
        pl.when(diag_low)(corner_copy.wait_send)
        pl.when(dom_up)(layer_force_copy.wait_send)
        pl.when(bin_up)(col_force_copy.wait_send)
        pl.when(diag_up)(corner_force_copy.wait_send)
        for i in range(1, NBIN):
            point_copy(i, parity).wait_send()

        def advance(x, carry):
            for p in range(3):
                at = pl.ds(pl.multiple_of(x * (ZT * CY), ZT * CY), ZT * CY)
                force = near[p, x] + far[p, x, :, 7:23, :]
                force = force + contact[p, at, :].reshape(ZT, CY, 128)
                moved = velo[p, x] + force * inverse[x]
                velo[p, x] = moved
                disp[p, x, :, 8:24, :] = disp[p, x, :, 8:24, :] + TIME_STEP * moved
            return carry

        lax.fori_loop(0, CX, advance, 0)
        return carry

    def point_copy(i, parity):
        return pltpu.make_async_remote_copy(
            src_ref=outgoing, dst_ref=pool.at[parity, own],
            send_sem=point_send.at[i - 1], recv_sem=point_recv.at[parity, i - 1],
            device_id=(dom, lax.rem(own + i, bins)), device_id_type=MESH,
        )

    lax.fori_loop(0, SUB, substep, 0)

    stores = []
    for z in range(ZT):
        z_at = pl.ds(z * 128, 128)
        stores.append((disp.at[:, pl.ds(0, CX), z, inner, :], disp_out.at[:, :, :, z_at]))
        stores.append((velo.at[:, :, z], velo_out.at[:, :, :, z_at]))
    stores = [pltpu.make_async_copy(a, b, out_sem.at[i]) for i, (a, b) in enumerate(stores)]
    for store in stores:
        store.start()

    device = dom * bins + own

    def split_tiles(x, carry):
        offset = tiles[x] - device * TILE_DEV + bins * TILE_DEV
        side = lax.shift_right_logical(offset, 10)
        row = side * 2 + (lax.shift_right_logical(offset, 7) & 1)
        at = pl.ds(pl.multiple_of(x * (ZT * CY), ZT * CY), ZT * CY)
        split_disp[at, 0:128] = row.astype(F32).astype(BF16).reshape(ZT * CY, 128)
        lane = (offset & 127).astype(F32).astype(BF16)
        split_disp[at, 128:256] = lane.reshape(ZT * CY, 128)
        return carry

    lax.fori_loop(0, CX, split_tiles, 0)

    def lay_heat(b, carry):
        at = pl.ds(pl.multiple_of(b * SEG, SEG), SEG)
        picked = jnp.dot(
            one_node[at, 0:ROWS], split_disp[0:ROWS, 0:256], preferred_element_type=F32
        )
        ids = lanes_of((SEG, SEG)).astype(F32)
        mask = lane_col[at, :] == ids
        row_col = jnp.sum(jnp.where(mask, picked[:, 0:128], 0.0), axis=1, keepdims=True)
        lane = jnp.sum(jnp.where(mask, picked[:, 128:256], 0.0), axis=1, keepdims=True)
        tile_row[b, 0:1, :] = jnp.sum(jnp.where(eye, row_col, 0.0), axis=0, keepdims=True)
        total = SHORT_GAIN * jnp.sum(heat_acc[at, :], axis=1, keepdims=True)
        laid = jnp.where(lane == ids, total, 0.0)
        for p, part in enumerate(pieces_of(laid)):
            tile_lane[p, at, :] = part
        return carry

    lax.fori_loop(0, NBLK, lay_heat, 0)
    on_tiles = jnp.zeros((16, 128), F32)
    for b in range(NBLK):
        ids = lax.broadcasted_iota(I32, (16, SEG), 0).astype(F32)
        hits = jnp.where(ids == tile_row[b, 0:1, :], 1.0, 0.0).astype(BF16)
        for p in range(PIECES):
            on_tiles = on_tiles + jnp.dot(
                hits, tile_lane[p, b * SEG : (b + 1) * SEG, :], preferred_element_type=F32
            )
    for side in range(3):
        heat_parts[side, 0:2, :] = on_tiles[side * 2 : side * 2 + 2, :]

    def heat_copy(index, to_dom):
        return pltpu.make_async_remote_copy(
            src_ref=heat_parts.at[2 * index], dst_ref=heat_in.at[index],
            send_sem=heat_send.at[index], recv_sem=heat_recv.at[index],
            device_id=(to_dom, own), device_id_type=MESH,
        )

    to_low, to_up = heat_copy(0, dom - 1), heat_copy(1, dom + 1)
    pl.when(dom_low)(to_low.start)
    pl.when(dom_up)(to_up.start)
    pl.when(dom_up)(to_low.wait_recv)
    pl.when(dom_low)(to_up.wait_recv)
    heat_out[...] = heat_parts[1, 0:2, :] + heat_in[0, 0:2, :] + heat_in[1, 0:2, :]
    pl.when(dom_low)(to_low.wait_send)
    pl.when(dom_up)(to_up.wait_send)
    for store in stores:
        store.wait()


def per_device(displacement, velocity, moduli, nodal_mass, node, base, contact_bin, element_tile):
    anywhere = pl.BlockSpec(memory_space=pl.ANY)
    vmem = pl.BlockSpec(memory_space=pltpu.VMEM)
    smem = pl.BlockSpec(memory_space=pltpu.SMEM)
    dma, vec = pltpu.SemaphoreType.DMA, pltpu.VMEM
    slab = (ZT, CY, 128)
    scratch = [
        vec((3, CX + 1, ZT, 32, 128), F32),
        vec((3, CX) + slab, F32),
        vec((2, CX) + slab, F32),
        vec((CX,) + slab, F32),
        vec((CX,) + slab, I32),
        vec((ROWS, PIECES * NSEG), BF16),
        vec((NSEG, PIECES * ROWS), BF16),
        vec((NSEG, 128), F32),
        vec((3, NSEG, 128), F32),
        vec((PIECES, NSEG, 128), BF16),
        vec((NBLK, 8, 128), F32),
        vec((PIECES * ROWS, 384), BF16),
        vec((PIECES * NSEG, 384), BF16),
        vec((3, NSEG, 128), F32),
        vec((NBLK + 1, 4, 128), F32),
        vec((NBIN * CAP, 4, 128), F32),
        vec((2, NBIN, NBIN * CAP, 4, 128), F32),
        vec((NBIN * NBIN * CAP, 3, 8, 128), F32),
        vec((3, NSEG, 128), F32),
        vec((NSEG, 128), F32),
        vec((3, ROWS, 128), F32),
        vec((3, 3, CX + 1) + slab, F32),
        vec((6, CX + 2) + slab, F32),
        vec((3, CX + 1) + slab, F32),
        vec((3, CX + 1, ZT, 32, 128), F32),
        vec((3, ZT, CX, 128), F32),
        vec((3, ZT, CX, 128), F32),
        vec((16, 128), F32),
        vec((16, 128), F32),
        vec((3,) + slab, F32),
        vec((3,) + slab, F32),
        vec((3, ZT, CX, 128), F32),
        vec((3, ZT, CX, 128), F32),
        vec((16, 128), F32),
        vec((16, 128), F32),
        vec((3, 8, 128), F32),
        vec((2, 8, 128), F32),
        pltpu.SMEM((SUB * NBIN * CAP,), I32),
        dma((5 * ZT,)),
        dma((2 * ZT,)),
        dma((6,)),
        dma((6,)),
        dma((NBIN - 1,)),
        dma((2, NBIN - 1)),
        dma((2,)),
        dma((2,)),
    ]
    new_displacement, new_velocity, heat = pl.pallas_call(
        kernel,
        out_shape=(
            jax.ShapeDtypeStruct(displacement.shape, F32),
            jax.ShapeDtypeStruct(velocity.shape, F32),
            jax.ShapeDtypeStruct((2, 128), F32),
        ),
        in_specs=[anywhere] * 5 + [vmem, vmem, smem],
        out_specs=(anywhere, anywhere, vmem),
        scratch_shapes=scratch,
        compiler_params=pltpu.CompilerParams(
            collective_id=0, has_side_effects=True, vmem_limit_bytes=56 << 20
        ),
        name="module_substeps",
    )(
        displacement, velocity, moduli, nodal_mass, element_tile,
        node.reshape(NBLK, SEG), base.reshape(3, NBLK, SEG), contact_bin.reshape(-1),
    )
    return new_displacement, new_velocity, heat.reshape(-1)


def solution(mesh):
    placed = (
        P(None, "dom", "bin", None),
        P(None, "dom", "bin", None),
        P(None, "dom", "bin", None),
        P("dom", "bin", None),
        P(("dom", "bin")),
        P(None, ("dom", "bin")),
        P(None, ("dom", "bin"), None),
        P("dom", "bin", None),
    )
    return jax.shard_map(
        per_device,
        mesh=mesh,
        in_specs=placed,
        out_specs=(P(None, "dom", "bin", None), P(None, "dom", "bin", None), P(("dom", "bin"))),
        check_vma=False,
    )
```

```python
import functools

import jax
import jax.numpy as jnp
from jax import lax
from jax.experimental import pallas as pl
from jax.experimental.pallas import tpu as pltpu
from jax.sharding import PartitionSpec as P

SUB = 4
SEG = 128
TILE_DEV = 256
RADIUS = 0.09
PENALTY = 4.0
SHORT_GAIN = 100.0
TIME_STEP = 0.2

CX, CY, ZT = 8, 16, 4
NBLK, CAP, NBIN = 8, 4, 4
NSEG = NBLK * SEG
ROWS = CX * ZT * CY
PIECES = 2
WIDE = 384
FAR = 1e12
MESH = pl.DeviceIdType.MESH
F32, BF16, I32 = jnp.float32, jnp.bfloat16, jnp.int32


def pieces_of(value):
    parts = []
    for _ in range(PIECES):
        part = value.astype(BF16)
        parts.append(part)
        value = value - part.astype(F32)
    return parts


def lanes_of(shape):
    return lax.broadcasted_iota(I32, shape, len(shape) - 1)


def next_z(value):
    turned = pltpu.roll(value, 127, 2)
    beyond = jnp.concatenate([turned[1:], turned[:1]], axis=0)
    return jnp.where(lanes_of(value.shape) == 127, beyond, turned)


def last_z(value):
    turned = pltpu.roll(value, 1, 2)
    before = jnp.concatenate([turned[-1:], turned[:-1]], axis=0)
    return jnp.where(lanes_of(value.shape) == 0, before, turned)


def spread_row(row):
    return jnp.broadcast_to(row, (SEG, SEG)).T


def kernel(
    disp_in, velo_in, moduli_in, mass_in, tile_in, node_ref, base_ref, bins_ref,
    disp_out, velo, heat_out,
    disp, moduli, inverse, tiles,
    one_seg, one_node, lane_col, base_col, tile_lane, tile_row,
    split_disp, split_push, seg_col, seg_row, outgoing, pool, spread,
    push_acc, heat_acc, picked, pushed,
    grads, stress, near, far,
    col_out, col_in, corner_out, corner_in,
    layer_force_out, layer_force_in, col_force_out, col_force_in,
    corner_force_out, corner_force_in,
    heat_parts, heat_in, slots,
    in_sem, send_sem, recv_sem, point_send, point_recv, heat_send, heat_recv,
):
    dom, own = lax.axis_index("dom"), lax.axis_index("bin")
    doms, bins = lax.axis_size("dom"), lax.axis_size("bin")
    dom_up, dom_low = dom < doms - 1, dom > 0
    bin_up, bin_low = own < bins - 1, own > 0
    diag_up, diag_low = jnp.logical_and(dom_up, bin_up), jnp.logical_and(dom_low, bin_low)

    loads = []
    for z in range(ZT):
        z_at = pl.ds(z * 128, 128)
        loads.append((disp_in.at[:, :, :, z_at], disp.at[:, pl.ds(0, CX), z, pl.ds(8, CY), :]))
        loads.append((tile_in.at[:, :, z_at], tiles.at[:, z]))
        loads.append((moduli_in.at[:, :, :, z_at], moduli.at[:, :, z]))
        loads.append((mass_in.at[:, :, z_at], inverse.at[:, z]))
        loads.append((velo_in.at[:, :, :, z_at], velo.at[:, :, z]))
    loads = [pltpu.make_async_copy(a, b, in_sem.at[i]) for i, (a, b) in enumerate(loads)]
    for load in loads:
        load.start()

    disp[:, CX, :, :, :] = jnp.zeros((3, ZT, 32, 128), F32)
    col_in[...] = jnp.zeros_like(col_in)
    corner_in[...] = jnp.zeros_like(corner_in)
    layer_force_in[...] = jnp.zeros_like(layer_force_in)
    col_force_in[...] = jnp.zeros_like(col_force_in)
    corner_force_in[...] = jnp.zeros_like(corner_force_in)
    heat_in[...] = jnp.zeros_like(heat_in)
    for k in range(6):
        stress[k, 0] = jnp.zeros((ZT, CY, 128), F32)
        stress[k, CX + 1] = jnp.zeros((ZT, CY, 128), F32)
    for p in range(3):
        far[p, CX, :, 0:8, :] = jnp.zeros((ZT, 8, 128), F32)
        seg_row[NBLK] = jnp.full((4, 128), FAR, F32)

    barrier = pltpu.get_barrier_semaphore()
    peers = [(dom, lax.rem(own + i, bins), None) for i in range(1, NBIN)]
    peers += [(dom + 1, own, dom_up), (dom - 1, own, dom_low)]
    peers += [(dom + 1, own + 1, diag_up), (dom - 1, own - 1, diag_low)]
    for to_dom, to_bin, exists in peers:
        def greet(to_dom=to_dom, to_bin=to_bin):
            pl.semaphore_signal(barrier, inc=1, device_id=(to_dom, to_bin), device_id_type=MESH)
        if exists is None:
            greet()
        else:
            pl.when(exists)(greet)

    def fill_slots(step, carry):
        named = [bins_ref[step, 0, b] for b in range(NBLK)]
        for k in range(NBIN):
            count = jnp.int32(0)
            found = [jnp.int32(NBLK)] * CAP
            for b in range(NBLK):
                same = named[b] == k
                for rank in range(CAP):
                    found[rank] = jnp.where(
                        jnp.logical_and(same, count == rank), jnp.int32(b), found[rank]
                    )
                count = count + same.astype(I32)
            for rank in range(CAP):
                slots[(step * NBIN + k) * CAP + rank] = found[rank]
        return carry

    lax.fori_loop(0, SUB, fill_slots, 0)

    eye = lax.broadcasted_iota(I32, (SEG, SEG), 0) == lanes_of((SEG, SEG))

    def place_block(b, carry):
        node = node_ref[pl.ds(b, 1), :]
        x, y = lax.shift_right_logical(node, 13), lax.shift_right_logical(node, 9) & 15
        z = lax.shift_right_logical(node, 7) & 3
        row = (x * ZT + z) * CY + y
        lane = node & 127
        at = pl.ds(pl.multiple_of(b * SEG, SEG), SEG)
        row_ids = lax.broadcasted_iota(I32, (ROWS, SEG), 0)
        one_seg[:, at] = jnp.where(row_ids == row, 1.0, 0.0).astype(BF16)
        row_col = spread_row(row.astype(F32))
        ids = lanes_of((SEG, SEG)).astype(F32)
        for part in range(ROWS // 128):
            hits = jnp.where(row_col == ids + float(128 * part), 1.0, 0.0).astype(BF16)
            one_node[at, part * 128 : part * 128 + 128] = hits
        lane_col[at, :] = spread_row(lane.astype(F32))
        for c in range(3):
            base_col[c, at, :] = spread_row(base_ref[c : c + 1, at])
        heat_acc[at, :] = jnp.zeros((SEG, SEG), F32)
        return carry

    lax.fori_loop(0, NBLK, place_block, 0)

    for load in loads:
        load.wait()

    def scale(x, carry):
        for k in range(2):
            moduli[k, x] = moduli[k, x] * -0.0625
        inverse[x] = TIME_STEP / inverse[x]
        return carry

    lax.fori_loop(0, CX, scale, 0)

    greeted = jnp.int32(NBIN - 1)
    for _, _, exists in peers[NBIN - 1 :]:
        greeted = greeted + exists.astype(I32)
    pl.semaphore_wait(barrier, greeted)

    def remote(src, dst, index, to_dom, to_bin):
        return pltpu.make_async_remote_copy(
            src_ref=src, dst_ref=dst, send_sem=send_sem.at[index], recv_sem=recv_sem.at[index],
            device_id=(to_dom, to_bin), device_id_type=MESH,
        )

    inner = pl.ds(8, CY)
    layer_copy = remote(disp.at[:, 0, :, inner, :], disp.at[:, CX, :, inner, :], 0, dom - 1, own)
    col_copy = remote(col_out, col_in, 1, dom, own - 1)
    corner_copy = remote(corner_out, corner_in, 2, dom - 1, own - 1)
    layer_force_copy = remote(layer_force_out, layer_force_in, 3, dom + 1, own)
    col_force_copy = remote(col_force_out, col_force_in, 4, dom, own + 1)
    corner_force_copy = remote(corner_force_out, corner_force_in, 5, dom + 1, own + 1)

    def touching(ahead, step, fresh):
        def rows_of(i, carry):
            at = pl.ds(pl.multiple_of(i * 16, 16), 16)
            mine = [seg_col[c, at, :].reshape(2, 8, 128) for c in range(3)]
            named = bins_ref[step, 0, i // 8]
            sums = [
                jnp.zeros((2, 8, 128), F32) if fresh else push_acc[c, at, :].reshape(2, 8, 128)
                for c in range(3)
            ]
            heat = heat_acc[at, :].reshape(2, 8, 128)
            for i in ahead:
                for k in range(CAP):
                    slot = i * (NBIN * CAP) + named * CAP + k
                    delta = [mine[c] - spread[slot, c] for c in range(3)]
                    square = delta[0] * delta[0] + delta[1] * delta[1] + delta[2] * delta[2]
                    square = jnp.maximum(square, 1e-30)
                    over = lax.rsqrt(square)
                    pressure = jnp.maximum(RADIUS - square * over, 0.0)
                    weight = pressure * jnp.minimum(over, 1.0 / (0.25 * RADIUS))
                    heat = heat + pressure * pressure
                    sums = [sums[c] + weight * delta[c] for c in range(3)]
            for c in range(3):
                push_acc[c, at, :] = sums[c].reshape(16, 128)
            heat_acc[at, :] = heat.reshape(16, 128)
            return carry

        lax.fori_loop(0, NSEG // 16, rows_of, 0)

    def substep(step, carry):
        parity = lax.rem(step, 2)

        for c in range(3):
            for z in range(ZT):
                corner_out[c * ZT + z : c * ZT + z + 1, :] = disp[c, 0, z, 8:9, :]
                for x in range(CX):
                    col_out[c, z, x : x + 1, :] = disp[c, x, z, 8:9, :]
        pl.when(dom_low)(layer_copy.start)
        pl.when(bin_low)(col_copy.start)
        pl.when(diag_low)(corner_copy.start)

        def split(pair, carry):
            for x in (2 * pair, 2 * pair + 1):
                at = pl.ds(pl.multiple_of(x * (ZT * CY), ZT * CY), ZT * CY)
                for c in range(3):
                    value = disp[c, x, :, 8 : 8 + CY, :].reshape(ZT * CY, 128)
                    for p, part in enumerate(pieces_of(value)):
                        split_disp[at, p * WIDE + c * 128 : p * WIDE + c * 128 + 128] = part
            return carry

        lax.fori_loop(0, CX // 2, split, 0)
        picked[...] = jnp.dot(one_node[...], split_disp[...], preferred_element_type=F32)

        def positions(pair, carry):
            for b in (2 * pair, 2 * pair + 1):
                at = pl.ds(pl.multiple_of(b * SEG, SEG), SEG)
                mask = lane_col[at, :] == lanes_of((SEG, SEG)).astype(F32)
                for c in range(3):
                    value = picked[at, c * 128 : c * 128 + 128]
                    value = value + picked[at, WIDE + c * 128 : WIDE + c * 128 + 128]
                    moved = jnp.where(mask, value, 0.0)
                    column = base_col[c, at, :] + jnp.sum(moved, axis=1, keepdims=True)
                    seg_col[c, at, :] = column
                    seg_row[b, c : c + 1, :] = jnp.sum(
                        jnp.where(eye, column, 0.0), axis=0, keepdims=True
                    )
            return carry

        lax.fori_loop(0, NBLK // 2, positions, 0)
        for slot in range(NBIN * CAP):
            block = seg_row[slots[step * (NBIN * CAP) + slot]]
            outgoing[slot] = block
            for c in range(3):
                spread[slot, c] = jnp.broadcast_to(block[c : c + 1, :], (8, 128))
        for i in range(1, NBIN):
            point_copy(i, parity).start()

        touching([0], step, True)

        pl.when(dom_up)(layer_copy.wait_recv)
        pl.when(bin_up)(col_copy.wait_recv)
        pl.when(diag_up)(corner_copy.wait_recv)
        for c in range(3):
            for z in range(ZT):
                disp[c, CX, z, 24:25, :] = corner_in[c * ZT + z : c * ZT + z + 1, :]
                for x in range(CX):
                    disp[c, x, z, 24:25, :] = col_in[c, z, x : x + 1, :]

        def corners(part, carry):
            for x in [3 * part + i for i in range(3)]:
                for c in range(3):
                    low, high = disp[c, x, :, 8:24, :], disp[c, x, :, 9:25, :]
                    total, gap = low + high, high - low
                    total_next, gap_next = next_z(total), next_z(gap)
                    grads[c, 0, x] = total + total_next
                    grads[c, 1, x] = gap + gap_next
                    grads[c, 2, x] = total_next - total
            return carry

        lax.fori_loop(0, (CX + 1) // 3, corners, 0)

        def stresses(x, carry):
            g = [
                [grads[c, 0, x + 1] - grads[c, 0, x]]
                + [grads[c, q, x] + grads[c, q, x + 1] for q in (1, 2)]
                for c in range(3)
            ]
            lame, shear = moduli[0, x], moduli[1, x]
            volume = lame * (g[0][0] + g[1][1] + g[2][2])
            for p in range(3):
                stress[p, x + 1] = shear * (g[p][p] + g[p][p]) + volume
            stress[3, x + 1] = shear * (g[0][1] + g[1][0])
            stress[4, x + 1] = shear * (g[0][2] + g[2][0])
            stress[5, x + 1] = shear * (g[1][2] + g[2][1])
            return carry

        lax.fori_loop(0, CX, stresses, 0)

        def forces(part, carry):
            for x in [3 * part + i for i in range(3)]:
                for p, (kx, ky, kz) in enumerate(((0, 3, 4), (3, 1, 5), (4, 5, 2))):
                    along_x = stress[kx, x] - stress[kx, x + 1]
                    along_y = stress[ky, x] + stress[ky, x + 1]
                    along_z = stress[kz, x] + stress[kz, x + 1]
                    minus, plus = along_x - along_y, along_x + along_y
                    near[p, x] = (minus - along_z) + last_z(minus + along_z)
                    far[p, x, :, 8:24, :] = (plus - along_z) + last_z(plus + along_z)
            return carry

        lax.fori_loop(0, (CX + 1) // 3, forces, 0)
        for p in range(3):
            layer_force_out[p] = near[p, CX] + far[p, CX, :, 7:23, :]
            for z in range(ZT):
                corner_force_out[p * ZT + z : p * ZT + z + 1, :] = far[p, CX, z, 23:24, :]
                for x in range(CX):
                    col_force_out[p, z, x : x + 1, :] = far[p, x, z, 23:24, :]
        pl.when(dom_up)(layer_force_copy.start)
        pl.when(bin_up)(col_force_copy.start)
        pl.when(diag_up)(corner_force_copy.start)

        for i in range(1, NBIN):
            point_copy(i, parity).wait_recv()

        def spread_slot(slot, carry):
            for i in range(1, NBIN):
                block = pool[parity, lax.rem(own + i, bins), slot]
                for c in range(3):
                    spread[i * (NBIN * CAP) + slot, c] = jnp.broadcast_to(
                        block[c : c + 1, :], (8, 128)
                    )
            return carry

        lax.fori_loop(0, NBIN * CAP, spread_slot, 0)
        touching(range(1, NBIN), step, False)

        def lay_push(pair, carry):
            for b in (2 * pair, 2 * pair + 1):
                at = pl.ds(pl.multiple_of(b * SEG, SEG), SEG)
                mask = lane_col[at, :] == lanes_of((SEG, SEG)).astype(F32)
                for c in range(3):
                    total = jnp.sum(push_acc[c, at, :], axis=1, keepdims=True)
                    laid = jnp.where(mask, PENALTY * total, 0.0)
                    for p, part in enumerate(pieces_of(laid)):
                        split_push[at, p * WIDE + c * 128 : p * WIDE + c * 128 + 128] = part
            return carry

        lax.fori_loop(0, NBLK // 2, lay_push, 0)
        pushed[...] = jnp.dot(one_seg[...], split_push[...], preferred_element_type=F32)

        pl.when(dom_low)(layer_force_copy.wait_recv)
        pl.when(bin_low)(col_force_copy.wait_recv)
        pl.when(diag_low)(corner_force_copy.wait_recv)
        for p in range(3):
            near[p, 0] = near[p, 0] + layer_force_in[p]
            for z in range(ZT):
                near[p, 0, z, 0:1, :] = (
                    near[p, 0, z, 0:1, :] + corner_force_in[p * ZT + z : p * ZT + z + 1, :]
                )
                for x in range(CX):
                    far[p, x, z, 7:8, :] = col_force_in[p, z, x : x + 1, :]
        pl.when(dom_low)(layer_copy.wait_send)
        pl.when(bin_low)(col_copy.wait_send)
        pl.when(diag_low)(corner_copy.wait_send)
        pl.when(dom_up)(layer_force_copy.wait_send)
        pl.when(bin_up)(col_force_copy.wait_send)
        pl.when(diag_up)(corner_force_copy.wait_send)
        for i in range(1, NBIN):
            point_copy(i, parity).wait_send()

        def advance(x, carry):
            for p in range(3):
                at = pl.ds(pl.multiple_of(x * (ZT * CY), ZT * CY), ZT * CY)
                force = near[p, x] + far[p, x, :, 7:23, :]
                for part in range(PIECES):
                    column = part * WIDE + p * 128
                    force = force + pushed[at, column : column + 128].reshape(ZT, CY, 128)
                moved = velo[p, x] + force * inverse[x]
                velo[p, x] = moved
                moved = disp[p, x, :, 8:24, :] + TIME_STEP * moved
                disp[p, x, :, 8:24, :] = moved
                disp_out[p, x] = moved
            return carry

        lax.fori_loop(0, CX, advance, 0)
        return carry

    def point_copy(i, parity):
        return pltpu.make_async_remote_copy(
            src_ref=outgoing, dst_ref=pool.at[parity, own],
            send_sem=point_send.at[i - 1], recv_sem=point_recv.at[parity, i - 1],
            device_id=(dom, lax.rem(own + i, bins)), device_id_type=MESH,
        )

    lax.fori_loop(0, SUB, substep, 0)

    device = dom * bins + own

    def split_tiles(x, carry):
        offset = tiles[x] - device * TILE_DEV + bins * TILE_DEV
        side = lax.shift_right_logical(offset, 10)
        row = side * 2 + (lax.shift_right_logical(offset, 7) & 1)
        at = pl.ds(pl.multiple_of(x * (ZT * CY), ZT * CY), ZT * CY)
        split_disp[at, 0:128] = row.astype(F32).astype(BF16).reshape(ZT * CY, 128)
        lane = (offset & 127).astype(F32).astype(BF16)
        split_disp[at, 128:256] = lane.reshape(ZT * CY, 128)
        return carry

    lax.fori_loop(0, CX, split_tiles, 0)

    def lay_heat(b, carry):
        at = pl.ds(pl.multiple_of(b * SEG, SEG), SEG)
        picked = jnp.dot(
            one_node[at, :], split_disp[:, 0:256], preferred_element_type=F32
        )
        ids = lanes_of((SEG, SEG)).astype(F32)
        mask = lane_col[at, :] == ids
        row_col = jnp.sum(jnp.where(mask, picked[:, 0:128], 0.0), axis=1, keepdims=True)
        lane = jnp.sum(jnp.where(mask, picked[:, 128:256], 0.0), axis=1, keepdims=True)
        tile_row[b, 0:1, :] = jnp.sum(jnp.where(eye, row_col, 0.0), axis=0, keepdims=True)
        total = SHORT_GAIN * jnp.sum(heat_acc[at, :], axis=1, keepdims=True)
        laid = jnp.where(lane == ids, total, 0.0)
        for p, part in enumerate(pieces_of(laid)):
            tile_lane[p, at, :] = part
        return carry

    lax.fori_loop(0, NBLK, lay_heat, 0)
    on_tiles = jnp.zeros((16, 128), F32)
    for b in range(NBLK):
        ids = lax.broadcasted_iota(I32, (16, SEG), 0).astype(F32)
        hits = jnp.where(ids == tile_row[b, 0:1, :], 1.0, 0.0).astype(BF16)
        for p in range(PIECES):
            on_tiles = on_tiles + jnp.dot(
                hits, tile_lane[p, b * SEG : (b + 1) * SEG, :], preferred_element_type=F32
            )
    for side in range(3):
        heat_parts[side, 0:2, :] = on_tiles[side * 2 : side * 2 + 2, :]

    def heat_copy(index, to_dom):
        return pltpu.make_async_remote_copy(
            src_ref=heat_parts.at[2 * index], dst_ref=heat_in.at[index],
            send_sem=heat_send.at[index], recv_sem=heat_recv.at[index],
            device_id=(to_dom, own), device_id_type=MESH,
        )

    to_low, to_up = heat_copy(0, dom - 1), heat_copy(1, dom + 1)
    pl.when(dom_low)(to_low.start)
    pl.when(dom_up)(to_up.start)
    pl.when(dom_up)(to_low.wait_recv)
    pl.when(dom_low)(to_up.wait_recv)
    heat_out[...] = heat_parts[1, 0:2, :] + heat_in[0, 0:2, :] + heat_in[1, 0:2, :]
    pl.when(dom_low)(to_low.wait_send)
    pl.when(dom_up)(to_up.wait_send)


def deliver(disp, velo, heat, disp_out, velo_out, heat_out, sem):
    stores = [(heat, heat_out)]
    for z in range(ZT):
        z_at = pl.ds(z * 128, 128)
        stores.append((disp.at[:, :, z], disp_out.at[:, :, :, z_at]))
        stores.append((velo.at[:, :, z], velo_out.at[:, :, :, z_at]))
    stores = [pltpu.make_async_copy(a, b, sem.at[i]) for i, (a, b) in enumerate(stores)]
    for store in stores:
        store.start()
    for store in stores:
        store.wait()


def per_device(displacement, velocity, moduli, nodal_mass, node, base, contact_bin, element_tile):
    anywhere = pl.BlockSpec(memory_space=pl.ANY)
    hbm = pl.BlockSpec(memory_space=pltpu.HBM)
    vmem = pl.BlockSpec(memory_space=pltpu.VMEM)
    smem = pl.BlockSpec(memory_space=pltpu.SMEM)
    dma, vec = pltpu.SemaphoreType.DMA, pltpu.VMEM
    slab = (ZT, CY, 128)
    scratch = [
        vec((3, CX + 1, ZT, 32, 128), F32),
        vec((2, CX) + slab, F32),
        vec((CX,) + slab, F32),
        vec((CX,) + slab, I32),
        vec((ROWS, NSEG), BF16),
        vec((NSEG, ROWS), BF16),
        vec((NSEG, 128), F32),
        vec((3, NSEG, 128), F32),
        vec((PIECES, NSEG, 128), BF16),
        vec((NBLK, 8, 128), F32),
        vec((ROWS, PIECES * WIDE), BF16),
        vec((NSEG, PIECES * WIDE), BF16),
        vec((3, NSEG, 128), F32),
        vec((NBLK + 1, 4, 128), F32),
        vec((NBIN * CAP, 4, 128), F32),
        vec((2, NBIN, NBIN * CAP, 4, 128), F32),
        vec((NBIN * NBIN * CAP, 3, 8, 128), F32),
        vec((3, NSEG, 128), F32),
        vec((NSEG, 128), F32),
        vec((NSEG, PIECES * WIDE), F32),
        vec((ROWS, PIECES * WIDE), F32),
        vec((3, 3, CX + 1) + slab, F32),
        vec((6, CX + 2) + slab, F32),
        vec((3, CX + 1) + slab, F32),
        vec((3, CX + 1, ZT, 32, 128), F32),
        vec((3, ZT, CX, 128), F32),
        vec((3, ZT, CX, 128), F32),
        vec((16, 128), F32),
        vec((16, 128), F32),
        vec((3,) + slab, F32),
        vec((3,) + slab, F32),
        vec((3, ZT, CX, 128), F32),
        vec((3, ZT, CX, 128), F32),
        vec((16, 128), F32),
        vec((16, 128), F32),
        vec((3, 8, 128), F32),
        vec((2, 8, 128), F32),
        pltpu.SMEM((SUB * NBIN * CAP,), I32),
        dma((5 * ZT,)),
        dma((6,)),
        dma((6,)),
        dma((NBIN - 1,)),
        dma((2, NBIN - 1)),
        dma((2,)),
        dma((2,)),
    ]
    results = pl.pallas_call(
        kernel,
        out_shape=(
            pltpu.VMEM((3, CX) + slab, F32),
            pltpu.VMEM((3, CX) + slab, F32),
            pltpu.VMEM((2, 128), F32),
        ),
        in_specs=[hbm] * 5 + [vmem, vmem, smem],
        out_specs=(vmem, vmem, vmem),
        scratch_shapes=scratch,
        compiler_params=pltpu.CompilerParams(
            collective_id=0, has_side_effects=True, vmem_limit_bytes=65339392
        ),
        name="module_substeps",
    )(
        displacement, velocity, moduli, nodal_mass, element_tile,
        node.reshape(NBLK, SEG), base, contact_bin.transpose(0, 2, 1),
    )
    new_displacement, new_velocity, heat = pl.pallas_call(
        deliver,
        out_shape=(
            jax.ShapeDtypeStruct(displacement.shape, F32),
            jax.ShapeDtypeStruct(velocity.shape, F32),
            jax.ShapeDtypeStruct((2, 128), F32),
        ),
        in_specs=[vmem] * 3,
        out_specs=(hbm, hbm, hbm),
        scratch_shapes=[dma((2 * ZT + 1,))],
        name="deliver",
    )(*[pltpu.with_memory_space_constraint(x, pltpu.VMEM) for x in results])
    return new_displacement, new_velocity, heat.reshape(-1)


def solution(mesh):
    placed = (
        P(None, "dom", "bin", None),
        P(None, "dom", "bin", None),
        P(None, "dom", "bin", None),
        P("dom", "bin", None),
        P(("dom", "bin")),
        P(None, ("dom", "bin")),
        P(None, ("dom", "bin"), None),
        P("dom", "bin", None),
    )
    return jax.shard_map(
        per_device,
        mesh=mesh,
        in_specs=placed,
        out_specs=(P(None, "dom", "bin", None), P(None, "dom", "bin", None), P(("dom", "bin"))),
        check_vma=False,
    )
```

```python
import functools

import jax
import jax.numpy as jnp
from jax import lax
from jax.experimental import pallas as pl
from jax.experimental.pallas import tpu as pltpu
from jax.sharding import PartitionSpec as P

SUB = 4
SEG = 128
TILE_DEV = 256
RADIUS = 0.09
PENALTY = 4.0
SHORT_GAIN = 100.0
TIME_STEP = 0.2

CX, CY, ZT = 8, 16, 4
NBLK, CAP, NBIN = 8, 4, 4
NSEG = NBLK * SEG
ROWS = CX * ZT * CY
PIECES = 2
ROWS_OWN, ROWS_OVER, ROWS_NEXT = 64, 64, 64
WIDE = 384
FAR = 1e12
NEXT, OVER, EMPTY = NBIN * CAP, 2 * NBIN * CAP, 3 * NBIN * CAP
MESH = pl.DeviceIdType.MESH
F32, BF16, I32 = jnp.float32, jnp.bfloat16, jnp.int32


def pieces_of(value):
    parts = []
    for _ in range(PIECES):
        part = value.astype(BF16)
        parts.append(part)
        value = value - part.astype(F32)
    return parts


def lanes_of(shape):
    return lax.broadcasted_iota(I32, shape, len(shape) - 1)


def next_z(value):
    turned = pltpu.roll(value, 127, 2)
    beyond = jnp.concatenate([turned[1:], turned[:1]], axis=0)
    return jnp.where(lanes_of(value.shape) == 127, beyond, turned)


def last_z(value):
    turned = pltpu.roll(value, 1, 2)
    before = jnp.concatenate([turned[-1:], turned[:-1]], axis=0)
    return jnp.where(lanes_of(value.shape) == 0, before, turned)


def spread_row(row):
    return jnp.broadcast_to(row, (SEG, SEG)).T


def kernel(
    disp_in, velo_in, moduli_in, mass_in, tile_in, node_ref, base_ref, bins_ref,
    disp_out, velo, heat_out,
    disp, moduli, inverse, tiles,
    one_seg, one_node, lane_col, base_col, tile_lane, tile_row,
    split_disp, split_push, seg_col, seg_row, outgoing, pool, spread,
    met_own, met_next, met_over, own_rows, return_out, return_in, heat_row,
    push_acc, heat_acc, picked, pushed,
    grads, stress, near, far,
    col_out, col_in, corner_out, corner_in,
    layer_force_out, layer_force_in, col_force_out, col_force_in,
    corner_force_out, corner_force_in,
    heat_parts, heat_in, slots, ranks,
    in_sem, send_sem, recv_sem, point_send, point_recv, return_send, return_recv,
    heat_send, heat_recv,
):
    dom, own = lax.axis_index("dom"), lax.axis_index("bin")
    doms, bins = lax.axis_size("dom"), lax.axis_size("bin")
    dom_up, dom_low = dom < doms - 1, dom > 0
    bin_up, bin_low = own < bins - 1, own > 0
    diag_up, diag_low = jnp.logical_and(dom_up, bin_up), jnp.logical_and(dom_low, bin_low)

    loads = []
    for z in range(ZT):
        z_at = pl.ds(z * 128, 128)
        loads.append((disp_in.at[:, :, :, z_at], disp.at[:, pl.ds(0, CX), z, pl.ds(8, CY), :]))
        loads.append((tile_in.at[:, :, z_at], tiles.at[:, z]))
        loads.append((moduli_in.at[:, :, :, z_at], moduli.at[:, :, z]))
        loads.append((mass_in.at[:, :, z_at], inverse.at[:, z]))
        loads.append((velo_in.at[:, :, :, z_at], velo.at[:, :, z]))
    loads = [pltpu.make_async_copy(a, b, in_sem.at[i]) for i, (a, b) in enumerate(loads)]
    for load in loads:
        load.start()

    disp[:, CX, :, :, :] = jnp.zeros((3, ZT, 32, 128), F32)
    col_in[...] = jnp.zeros_like(col_in)
    corner_in[...] = jnp.zeros_like(corner_in)
    layer_force_in[...] = jnp.zeros_like(layer_force_in)
    col_force_in[...] = jnp.zeros_like(col_force_in)
    corner_force_in[...] = jnp.zeros_like(corner_force_in)
    heat_in[...] = jnp.zeros_like(heat_in)
    for k in range(6):
        stress[k, 0] = jnp.zeros((ZT, CY, 128), F32)
        stress[k, CX + 1] = jnp.zeros((ZT, CY, 128), F32)
    for p in range(3):
        far[p, CX, :, 0:8, :] = jnp.zeros((ZT, 8, 128), F32)
        spread[EMPTY, p] = jnp.full((8, 128), FAR, F32)
    seg_row[NBLK] = jnp.full((4, 128), FAR, F32)
    met_own[NBLK] = jnp.zeros((2, 4, 8, 128), F32)
    met_next[NBLK] = jnp.zeros((4, 4, 8, 128), F32)
    met_over[NBLK] = jnp.zeros((2, 4, 8, 128), F32)
    heat_row[...] = jnp.zeros_like(heat_row)

    barrier = pltpu.get_barrier_semaphore()
    peers = [(dom, lax.rem(own + i, bins), None) for i in range(1, NBIN)]
    peers += [(dom + 1, own, dom_up), (dom - 1, own, dom_low)]
    peers += [(dom + 1, own + 1, diag_up), (dom - 1, own - 1, diag_low)]
    for to_dom, to_bin, exists in peers:
        def greet(to_dom=to_dom, to_bin=to_bin):
            pl.semaphore_signal(barrier, inc=1, device_id=(to_dom, to_bin), device_id_type=MESH)
        if exists is None:
            greet()
        else:
            pl.when(exists)(greet)

    def fill_slots(step, carry):
        named = [bins_ref[step, 0, b] for b in range(NBLK)]
        for b in range(NBLK):
            rank = jnp.int32(0)
            for before in range(b):
                rank = rank + (named[before] == named[b]).astype(I32)
            ranks[step * NBLK + b] = rank
        for k in range(NBIN):
            count = jnp.int32(0)
            found = [jnp.int32(NBLK)] * CAP
            for b in range(NBLK):
                same = named[b] == k
                for rank in range(CAP):
                    found[rank] = jnp.where(
                        jnp.logical_and(same, count == rank), jnp.int32(b), found[rank]
                    )
                count = count + same.astype(I32)
            for rank in range(CAP):
                slots[(step * NBIN + k) * CAP + rank] = found[rank]
        return carry

    lax.fori_loop(0, SUB, fill_slots, 0)

    eye = lax.broadcasted_iota(I32, (SEG, SEG), 0) == lanes_of((SEG, SEG))

    def place_block(b, carry):
        node = node_ref[pl.ds(b, 1), :]
        x, y = lax.shift_right_logical(node, 13), lax.shift_right_logical(node, 9) & 15
        z = lax.shift_right_logical(node, 7) & 3
        row = (x * ZT + z) * CY + y
        lane = node & 127
        at = pl.ds(pl.multiple_of(b * SEG, SEG), SEG)
        row_ids = lax.broadcasted_iota(I32, (ROWS, SEG), 0)
        one_seg[:, at] = jnp.where(row_ids == row, 1.0, 0.0).astype(BF16)
        row_col = spread_row(row.astype(F32))
        ids = lanes_of((SEG, SEG)).astype(F32)
        for part in range(ROWS // 128):
            hits = jnp.where(row_col == ids + float(128 * part), 1.0, 0.0).astype(BF16)
            one_node[at, part * 128 : part * 128 + 128] = hits
        lane_col[at, :] = spread_row(lane.astype(F32))
        for c in range(3):
            base_col[c, at, :] = spread_row(base_ref[c : c + 1, at])
        heat_acc[at, :] = jnp.zeros((SEG, SEG), F32)
        return carry

    lax.fori_loop(0, NBLK, place_block, 0)

    for load in loads:
        load.wait()

    def scale(x, carry):
        for k in range(2):
            moduli[k, x] = moduli[k, x] * -0.0625
        inverse[x] = TIME_STEP / inverse[x]
        return carry

    lax.fori_loop(0, CX, scale, 0)

    greeted = jnp.int32(NBIN - 1)
    for _, _, exists in peers[NBIN - 1 :]:
        greeted = greeted + exists.astype(I32)
    pl.semaphore_wait(barrier, greeted)

    def remote(src, dst, index, to_dom, to_bin):
        return pltpu.make_async_remote_copy(
            src_ref=src, dst_ref=dst, send_sem=send_sem.at[index], recv_sem=recv_sem.at[index],
            device_id=(to_dom, to_bin), device_id_type=MESH,
        )

    inner = pl.ds(8, CY)
    layer_copy = remote(disp.at[:, 0, :, inner, :], disp.at[:, CX, :, inner, :], 0, dom - 1, own)
    col_copy = remote(col_out, col_in, 1, dom, own - 1)
    corner_copy = remote(corner_out, corner_in, 2, dom - 1, own - 1)
    layer_force_copy = remote(layer_force_out, layer_force_in, 3, dom + 1, own)
    col_force_copy = remote(col_force_out, col_force_in, 4, dom, own + 1)
    corner_force_copy = remote(corner_force_out, corner_force_in, 5, dom + 1, own + 1)

    def touching(step, slots_of, met, rows, itself):
        def with_block(b, carry):
            facing = slots_of(bins_ref[step, 0, b], ranks[step * NBLK + b])

            def with_rows(g, met_sums):
                met_sums = [list(each) for each in met_sums]
                at = pl.ds(pl.multiple_of(b * SEG + g * rows, rows), rows)
                wide = (rows // 8, 8, 128)
                mine = [seg_col[c, at, :].reshape(wide) for c in range(3)]
                if itself:
                    sums = [jnp.zeros(wide, F32) for c in range(3)]
                else:
                    sums = [push_acc[c, at, :].reshape(wide) for c in range(3)]
                heat = heat_acc[at, :].reshape(wide)
                for j, slot in enumerate(facing):
                    delta = [mine[c] - spread[slot, c] for c in range(3)]
                    square = delta[0] * delta[0] + delta[1] * delta[1] + delta[2] * delta[2]
                    square = jnp.maximum(square, 1e-30)
                    over = lax.rsqrt(square)
                    pressure = jnp.maximum(RADIUS - square * over, 0.0)
                    weight = pressure * jnp.minimum(over, 1.0 / (0.25 * RADIUS))
                    parts = [weight * delta[c] for c in range(3)] + [pressure * pressure]
                    sums = [sums[c] + parts[c] for c in range(3)]
                    heat = heat + parts[3]
                    if itself and j == 0:
                        continue
                    row = met_sums[j - itself]
                    for q in range(4):
                        row[q] = row[q] + jnp.sum(parts[q], axis=0)
                for c in range(3):
                    push_acc[c, at, :] = sums[c].reshape(rows, 128)
                heat_acc[at, :] = heat.reshape(rows, 128)
                return met_sums

            none = [[jnp.zeros((8, 128), F32)] * 4 for _ in facing[itself:]]
            met_sums = lax.fori_loop(0, SEG // rows, with_rows, none)
            for j, each in enumerate(met_sums):
                for q in range(4):
                    met[b, j, q] = each[q]
            return carry

        lax.fori_loop(0, NBLK, with_block, 0)

    high = (own >= NBIN // 2).astype(I32)

    def own_slots(named, rank):
        base = named * CAP
        opposite = jnp.where(rank < CAP // 2, base + ((rank + 2) & (CAP - 1)), EMPTY)
        return [base + rank, base + ((rank + 1) & (CAP - 1)), opposite]

    def next_slots(named, rank):
        return [NEXT + named * CAP + k for k in range(CAP)]

    def over_slots(named, rank):
        first = OVER + named * CAP + ((rank + high) & 1)
        return [first, first + 2]

    def rows_of(values):
        return jnp.sum(functools.reduce(lambda a, b: a + b, values), axis=0, keepdims=True)

    def substep(step, carry):
        for c in range(3):
            for z in range(ZT):
                corner_out[c * ZT + z : c * ZT + z + 1, :] = disp[c, 0, z, 8:9, :]
                for x in range(CX):
                    col_out[c, z, x : x + 1, :] = disp[c, x, z, 8:9, :]
        pl.when(dom_low)(layer_copy.start)
        pl.when(bin_low)(col_copy.start)
        pl.when(diag_low)(corner_copy.start)

        def split(pair, carry):
            for x in (2 * pair, 2 * pair + 1):
                at = pl.ds(pl.multiple_of(x * (ZT * CY), ZT * CY), ZT * CY)
                for c in range(3):
                    value = disp[c, x, :, 8 : 8 + CY, :].reshape(ZT * CY, 128)
                    for p, part in enumerate(pieces_of(value)):
                        split_disp[at, p * WIDE + c * 128 : p * WIDE + c * 128 + 128] = part
            return carry

        lax.fori_loop(0, CX // 2, split, 0)
        picked[...] = jnp.dot(one_node[...], split_disp[...], preferred_element_type=F32)

        def positions(pair, carry):
            for b in (2 * pair, 2 * pair + 1):
                at = pl.ds(pl.multiple_of(b * SEG, SEG), SEG)
                mask = lane_col[at, :] == lanes_of((SEG, SEG)).astype(F32)
                for c in range(3):
                    value = picked[at, c * 128 : c * 128 + 128]
                    value = value + picked[at, WIDE + c * 128 : WIDE + c * 128 + 128]
                    moved = jnp.where(mask, value, 0.0)
                    column = base_col[c, at, :] + jnp.sum(moved, axis=1, keepdims=True)
                    seg_col[c, at, :] = column
                    seg_row[b, c : c + 1, :] = jnp.sum(
                        jnp.where(eye, column, 0.0), axis=0, keepdims=True
                    )
            return carry

        lax.fori_loop(0, NBLK // 2, positions, 0)
        for slot in range(NBIN * CAP):
            block = seg_row[slots[step * (NBIN * CAP) + slot]]
            outgoing[slot] = block
            for c in range(3):
                spread[slot, c] = jnp.broadcast_to(block[c : c + 1, :], (8, 128))
        for i in range(2):
            point_copy(i).start()

        touching(step, own_slots, met_own, ROWS_OWN, 1)

        def gather_own(k, carry):
            named = [slots[step * (NBIN * CAP) + k * CAP + r] for r in range(CAP)]
            for r in range(CAP):
                for q in range(4):
                    values = [met_own[named[(r + 3) % CAP], 0, q]]
                    if r >= CAP // 2:
                        values.append(met_own[named[r - CAP // 2], 1, q])
                    own_rows[k * CAP + r, q : q + 1, :] = rows_of(values)
            return carry

        lax.fori_loop(0, NBIN, gather_own, 0)

        pl.when(dom_up)(layer_copy.wait_recv)
        pl.when(bin_up)(col_copy.wait_recv)
        pl.when(diag_up)(corner_copy.wait_recv)
        for c in range(3):
            for z in range(ZT):
                disp[c, CX, z, 24:25, :] = corner_in[c * ZT + z : c * ZT + z + 1, :]
                for x in range(CX):
                    disp[c, x, z, 24:25, :] = col_in[c, z, x : x + 1, :]

        def corners(part, carry):
            for x in [3 * part + i for i in range(3)]:
                for c in range(3):
                    low, high = disp[c, x, :, 8:24, :], disp[c, x, :, 9:25, :]
                    total, gap = low + high, high - low
                    total_next, gap_next = next_z(total), next_z(gap)
                    grads[c, 0, x] = total + total_next
                    grads[c, 1, x] = gap + gap_next
                    grads[c, 2, x] = total_next - total
            return carry

        lax.fori_loop(0, (CX + 1) // 3, corners, 0)

        def stresses(x, carry):
            g = [
                [grads[c, 0, x + 1] - grads[c, 0, x]]
                + [grads[c, q, x] + grads[c, q, x + 1] for q in (1, 2)]
                for c in range(3)
            ]
            lame, shear = moduli[0, x], moduli[1, x]
            volume = lame * (g[0][0] + g[1][1] + g[2][2])
            for p in range(3):
                stress[p, x + 1] = shear * (g[p][p] + g[p][p]) + volume
            stress[3, x + 1] = shear * (g[0][1] + g[1][0])
            stress[4, x + 1] = shear * (g[0][2] + g[2][0])
            stress[5, x + 1] = shear * (g[1][2] + g[2][1])
            return carry

        lax.fori_loop(0, CX, stresses, 0)

        def spread_from(i):
            point_copy(i).wait_recv()

            def spread_slot(slot, carry):
                block = pool[i, slot]
                for c in range(3):
                    spread[NEXT * (i + 1) + slot, c] = jnp.broadcast_to(
                        block[c : c + 1, :], (8, 128)
                    )
                return carry

            lax.fori_loop(0, NBIN * CAP, spread_slot, 0)

        spread_from(1)
        touching(step, over_slots, met_over, ROWS_OVER, 0)

        def gather_over(k, carry):
            for r in range(CAP):
                first = step * (NBIN * CAP) + k * CAP + ((r + high) & 1)
                named = [slots[first], slots[first + 2]]
                for q in range(4):
                    values = [met_over[each, r // 2, q] for each in named]
                    return_out[1, k * CAP + r, q : q + 1, :] = rows_of(values)
            return carry

        lax.fori_loop(0, NBIN, gather_over, 0)
        return_copy(1).start()
        spread_from(0)
        touching(step, next_slots, met_next, ROWS_NEXT, 0)

        def gather_next(k, carry):
            named = [slots[step * (NBIN * CAP) + k * CAP + r] for r in range(CAP)]
            for r in range(CAP):
                for q in range(4):
                    values = [met_next[each, r, q] for each in named]
                    return_out[0, k * CAP + r, q : q + 1, :] = rows_of(values)
            return carry

        lax.fori_loop(0, NBIN, gather_next, 0)
        return_copy(0).start()

        def forces(part, carry):
            for x in [3 * part + i for i in range(3)]:
                for p, (kx, ky, kz) in enumerate(((0, 3, 4), (3, 1, 5), (4, 5, 2))):
                    along_x = stress[kx, x] - stress[kx, x + 1]
                    along_y = stress[ky, x] + stress[ky, x + 1]
                    along_z = stress[kz, x] + stress[kz, x + 1]
                    minus, plus = along_x - along_y, along_x + along_y
                    near[p, x] = (minus - along_z) + last_z(minus + along_z)
                    far[p, x, :, 8:24, :] = (plus - along_z) + last_z(plus + along_z)
            return carry

        lax.fori_loop(0, (CX + 1) // 3, forces, 0)
        for p in range(3):
            layer_force_out[p] = near[p, CX] + far[p, CX, :, 7:23, :]
            for z in range(ZT):
                corner_force_out[p * ZT + z : p * ZT + z + 1, :] = far[p, CX, z, 23:24, :]
                for x in range(CX):
                    col_force_out[p, z, x : x + 1, :] = far[p, x, z, 23:24, :]
        pl.when(dom_up)(layer_force_copy.start)
        pl.when(bin_up)(col_force_copy.start)
        pl.when(diag_up)(corner_force_copy.start)

        for i in range(2):
            return_copy(i).wait_recv()

        def lay_push(pair, carry):
            for b in (2 * pair, 2 * pair + 1):
                at = pl.ds(pl.multiple_of(b * SEG, SEG), SEG)
                mask = lane_col[at, :] == lanes_of((SEG, SEG)).astype(F32)
                slot = bins_ref[step, 0, b] * CAP + ranks[step * NBLK + b]
                met = own_rows[slot] + return_in[0, slot] + return_in[1, slot]
                heat_row[b] = heat_row[b] + met[3:4, :]
                for c in range(3):
                    total = push_acc[c, at, :] - jnp.where(eye, met[c : c + 1, :], 0.0)
                    total = jnp.sum(total, axis=1, keepdims=True)
                    laid = jnp.where(mask, PENALTY * total, 0.0)
                    for p, part in enumerate(pieces_of(laid)):
                        split_push[at, p * WIDE + c * 128 : p * WIDE + c * 128 + 128] = part
            return carry

        lax.fori_loop(0, NBLK // 2, lay_push, 0)
        pushed[...] = jnp.dot(one_seg[...], split_push[...], preferred_element_type=F32)

        pl.when(dom_low)(layer_force_copy.wait_recv)
        pl.when(bin_low)(col_force_copy.wait_recv)
        pl.when(diag_low)(corner_force_copy.wait_recv)
        for p in range(3):
            near[p, 0] = near[p, 0] + layer_force_in[p]
            for z in range(ZT):
                near[p, 0, z, 0:1, :] = (
                    near[p, 0, z, 0:1, :] + corner_force_in[p * ZT + z : p * ZT + z + 1, :]
                )
                for x in range(CX):
                    far[p, x, z, 7:8, :] = col_force_in[p, z, x : x + 1, :]
        pl.when(dom_low)(layer_copy.wait_send)
        pl.when(bin_low)(col_copy.wait_send)
        pl.when(diag_low)(corner_copy.wait_send)
        pl.when(dom_up)(layer_force_copy.wait_send)
        pl.when(bin_up)(col_force_copy.wait_send)
        pl.when(diag_up)(corner_force_copy.wait_send)
        for i in range(2):
            point_copy(i).wait_send()
            return_copy(i).wait_send()

        def advance(x, carry):
            for p in range(3):
                at = pl.ds(pl.multiple_of(x * (ZT * CY), ZT * CY), ZT * CY)
                force = near[p, x] + far[p, x, :, 7:23, :]
                for part in range(PIECES):
                    column = part * WIDE + p * 128
                    force = force + pushed[at, column : column + 128].reshape(ZT, CY, 128)
                moved = velo[p, x] + force * inverse[x]
                velo[p, x] = moved
                moved = disp[p, x, :, 8:24, :] + TIME_STEP * moved
                disp[p, x, :, 8:24, :] = moved
                disp_out[p, x] = moved
            return carry

        lax.fori_loop(0, CX, advance, 0)
        return carry

    def point_copy(i):
        return pltpu.make_async_remote_copy(
            src_ref=outgoing, dst_ref=pool.at[i],
            send_sem=point_send.at[i], recv_sem=point_recv.at[i],
            device_id=(dom, lax.rem(own + bins - 1 - i, bins)), device_id_type=MESH,
        )

    def return_copy(i):
        return pltpu.make_async_remote_copy(
            src_ref=return_out.at[i], dst_ref=return_in.at[i],
            send_sem=return_send.at[i], recv_sem=return_recv.at[i],
            device_id=(dom, lax.rem(own + 1 + i, bins)), device_id_type=MESH,
        )

    lax.fori_loop(0, SUB, substep, 0)

    device = dom * bins + own

    def split_tiles(x, carry):
        offset = tiles[x] - device * TILE_DEV + bins * TILE_DEV
        side = lax.shift_right_logical(offset, 10)
        row = side * 2 + (lax.shift_right_logical(offset, 7) & 1)
        at = pl.ds(pl.multiple_of(x * (ZT * CY), ZT * CY), ZT * CY)
        split_disp[at, 0:128] = row.astype(F32).astype(BF16).reshape(ZT * CY, 128)
        lane = (offset & 127).astype(F32).astype(BF16)
        split_disp[at, 128:256] = lane.reshape(ZT * CY, 128)
        return carry

    lax.fori_loop(0, CX, split_tiles, 0)

    def lay_heat(b, carry):
        at = pl.ds(pl.multiple_of(b * SEG, SEG), SEG)
        picked = jnp.dot(
            one_node[at, :], split_disp[:, 0:256], preferred_element_type=F32
        )
        ids = lanes_of((SEG, SEG)).astype(F32)
        mask = lane_col[at, :] == ids
        row_col = jnp.sum(jnp.where(mask, picked[:, 0:128], 0.0), axis=1, keepdims=True)
        lane = jnp.sum(jnp.where(mask, picked[:, 128:256], 0.0), axis=1, keepdims=True)
        tile_row[b, 0:1, :] = jnp.sum(jnp.where(eye, row_col, 0.0), axis=0, keepdims=True)
        total = heat_acc[at, :] + jnp.where(eye, heat_row[b], 0.0)
        total = SHORT_GAIN * jnp.sum(total, axis=1, keepdims=True)
        laid = jnp.where(lane == ids, total, 0.0)
        for p, part in enumerate(pieces_of(laid)):
            tile_lane[p, at, :] = part
        return carry

    lax.fori_loop(0, NBLK, lay_heat, 0)
    on_tiles = jnp.zeros((16, 128), F32)
    for b in range(NBLK):
        ids = lax.broadcasted_iota(I32, (16, SEG), 0).astype(F32)
        hits = jnp.where(ids == tile_row[b, 0:1, :], 1.0, 0.0).astype(BF16)
        for p in range(PIECES):
            on_tiles = on_tiles + jnp.dot(
                hits, tile_lane[p, b * SEG : (b + 1) * SEG, :], preferred_element_type=F32
            )
    for side in range(3):
        heat_parts[side, 0:2, :] = on_tiles[side * 2 : side * 2 + 2, :]

    def heat_copy(index, to_dom):
        return pltpu.make_async_remote_copy(
            src_ref=heat_parts.at[2 * index], dst_ref=heat_in.at[index],
            send_sem=heat_send.at[index], recv_sem=heat_recv.at[index],
            device_id=(to_dom, own), device_id_type=MESH,
        )

    to_low, to_up = heat_copy(0, dom - 1), heat_copy(1, dom + 1)
    pl.when(dom_low)(to_low.start)
    pl.when(dom_up)(to_up.start)
    pl.when(dom_up)(to_low.wait_recv)
    pl.when(dom_low)(to_up.wait_recv)
    heat_out[...] = heat_parts[1, 0:2, :] + heat_in[0, 0:2, :] + heat_in[1, 0:2, :]
    pl.when(dom_low)(to_low.wait_send)
    pl.when(dom_up)(to_up.wait_send)


def deliver(disp, velo, heat, disp_out, velo_out, heat_out, sem):
    stores = [(heat, heat_out)]
    for z in range(ZT):
        z_at = pl.ds(z * 128, 128)
        stores.append((disp.at[:, :, z], disp_out.at[:, :, :, z_at]))
        stores.append((velo.at[:, :, z], velo_out.at[:, :, :, z_at]))
    stores = [pltpu.make_async_copy(a, b, sem.at[i]) for i, (a, b) in enumerate(stores)]
    for store in stores:
        store.start()
    for store in stores:
        store.wait()


def per_device(displacement, velocity, moduli, nodal_mass, node, base, contact_bin, element_tile):
    anywhere = pl.BlockSpec(memory_space=pl.ANY)
    hbm = pl.BlockSpec(memory_space=pltpu.HBM)
    vmem = pl.BlockSpec(memory_space=pltpu.VMEM)
    smem = pl.BlockSpec(memory_space=pltpu.SMEM)
    dma, vec = pltpu.SemaphoreType.DMA, pltpu.VMEM
    slab = (ZT, CY, 128)
    scratch = [
        vec((3, CX + 1, ZT, 32, 128), F32),
        vec((2, CX) + slab, F32),
        vec((CX,) + slab, F32),
        vec((CX,) + slab, I32),
        vec((ROWS, NSEG), BF16),
        vec((NSEG, ROWS), BF16),
        vec((NSEG, 128), F32),
        vec((3, NSEG, 128), F32),
        vec((PIECES, NSEG, 128), BF16),
        vec((NBLK, 8, 128), F32),
        vec((ROWS, PIECES * WIDE), BF16),
        vec((NSEG, PIECES * WIDE), BF16),
        vec((3, NSEG, 128), F32),
        vec((NBLK + 1, 4, 128), F32),
        vec((NBIN * CAP, 4, 128), F32),
        vec((2, NBIN * CAP, 4, 128), F32),
        vec((3 * NBIN * CAP + 1, 3, 8, 128), F32),
        vec((NBLK + 1, 2, 4, 8, 128), F32),
        vec((NBLK + 1, 4, 4, 8, 128), F32),
        vec((NBLK + 1, 2, 4, 8, 128), F32),
        vec((NBIN * CAP, 4, 128), F32),
        vec((2, NBIN * CAP, 4, 128), F32),
        vec((2, NBIN * CAP, 4, 128), F32),
        vec((NBLK, 1, 128), F32),
        vec((3, NSEG, 128), F32),
        vec((NSEG, 128), F32),
        vec((NSEG, PIECES * WIDE), F32),
        vec((ROWS, PIECES * WIDE), F32),
        vec((3, 3, CX + 1) + slab, F32),
        vec((6, CX + 2) + slab, F32),
        vec((3, CX + 1) + slab, F32),
        vec((3, CX + 1, ZT, 32, 128), F32),
        vec((3, ZT, CX, 128), F32),
        vec((3, ZT, CX, 128), F32),
        vec((16, 128), F32),
        vec((16, 128), F32),
        vec((3,) + slab, F32),
        vec((3,) + slab, F32),
        vec((3, ZT, CX, 128), F32),
        vec((3, ZT, CX, 128), F32),
        vec((16, 128), F32),
        vec((16, 128), F32),
        vec((3, 8, 128), F32),
        vec((2, 8, 128), F32),
        pltpu.SMEM((SUB * NBIN * CAP,), I32),
        pltpu.SMEM((SUB * NBLK,), I32),
        dma((5 * ZT,)),
        dma((6,)),
        dma((6,)),
        dma((2,)),
        dma((2,)),
        dma((2,)),
        dma((2,)),
        dma((2,)),
        dma((2,)),
    ]
    results = pl.pallas_call(
        kernel,
        out_shape=(
            pltpu.VMEM((3, CX) + slab, F32),
            pltpu.VMEM((3, CX) + slab, F32),
            pltpu.VMEM((2, 128), F32),
        ),
        in_specs=[hbm] * 5 + [vmem, vmem, smem],
        out_specs=(vmem, vmem, vmem),
        scratch_shapes=scratch,
        compiler_params=pltpu.CompilerParams(
            collective_id=0, has_side_effects=True, vmem_limit_bytes=65339392
        ),
        name="module_substeps",
    )(
        displacement, velocity, moduli, nodal_mass, element_tile,
        node.reshape(NBLK, SEG), base, contact_bin.transpose(0, 2, 1),
    )
    new_displacement, new_velocity, heat = pl.pallas_call(
        deliver,
        out_shape=(
            jax.ShapeDtypeStruct(displacement.shape, F32),
            jax.ShapeDtypeStruct(velocity.shape, F32),
            jax.ShapeDtypeStruct((2, 128), F32),
        ),
        in_specs=[vmem] * 3,
        out_specs=(hbm, hbm, hbm),
        scratch_shapes=[dma((2 * ZT + 1,))],
        name="deliver",
    )(*[pltpu.with_memory_space_constraint(x, pltpu.VMEM) for x in results])
    return new_displacement, new_velocity, heat.reshape(-1)


def solution(mesh):
    placed = (
        P(None, "dom", "bin", None),
        P(None, "dom", "bin", None),
        P(None, "dom", "bin", None),
        P("dom", "bin", None),
        P(("dom", "bin")),
        P(None, ("dom", "bin")),
        P(None, ("dom", "bin"), None),
        P("dom", "bin", None),
    )
    return jax.shard_map(
        per_device,
        mesh=mesh,
        in_specs=placed,
        out_specs=(P(None, "dom", "bin", None), P(None, "dom", "bin", None), P(("dom", "bin"))),
        check_vma=False,
    )
```

```python
import functools

import jax
import jax.numpy as jnp
from jax import lax
from jax.experimental import pallas as pl
from jax.experimental.pallas import tpu as pltpu
from jax.sharding import PartitionSpec as P

SUB = 4
SEG = 128
TILE_DEV = 256
RADIUS = 0.09
PENALTY = 4.0
SHORT_GAIN = 100.0
TIME_STEP = 0.2

CX, CY, ZT = 8, 16, 4
NBLK, CAP, NBIN = 8, 4, 4
NSEG = NBLK * SEG
ROWS = CX * ZT * CY
PIECES = 2
ROWS_OWN, ROWS_OVER, ROWS_NEXT = 64, 64, 64
WIDE = 384
FAR = 1e12
BINS = SUB * NBIN * CAP
RANKS = BINS + SUB * NBLK
TABLE = RANKS + SUB * NBLK
NEXT, OVER, LAST = NBLK + 1, 2 * (NBLK + 1), 3 * (NBLK + 1)
MESH = pl.DeviceIdType.MESH
F32, BF16, I32 = jnp.float32, jnp.bfloat16, jnp.int32


def pieces_of(value):
    parts = []
    for _ in range(PIECES):
        part = value.astype(BF16)
        parts.append(part)
        value = value - part.astype(F32)
    return parts


def lanes_of(shape):
    return lax.broadcasted_iota(I32, shape, len(shape) - 1)


def next_z(value):
    turned = pltpu.roll(value, 127, 2)
    beyond = jnp.concatenate([turned[1:], turned[:1]], axis=0)
    return jnp.where(lanes_of(value.shape) == 127, beyond, turned)


def last_z(value):
    turned = pltpu.roll(value, 1, 2)
    before = jnp.concatenate([turned[-1:], turned[:-1]], axis=0)
    return jnp.where(lanes_of(value.shape) == 0, before, turned)


def spread_row(row):
    return jnp.broadcast_to(row, (SEG, SEG)).T


def kernel(
    disp_in, velo_in, moduli_in, mass_in, tile_in, node_ref, base_ref, bins_ref,
    disp_out, velo, heat_out,
    disp, moduli, inverse, tiles,
    one_seg, one_node, lane_col, base_col, tile_lane, tile_row,
    split_disp, split_push, seg_col, seg_row, pool, spread,
    met_own, met_over, own_rows, return_out, return_in, heat_row,
    push_acc, heat_acc, picked, pushed,
    grads, stress, near, far,
    col_out, col_in, corner_out, corner_in,
    layer_force_out, layer_force_in, col_force_out, col_force_in,
    corner_force_out, corner_force_in,
    heat_parts, heat_in, table, tables,
    in_sem, send_sem, recv_sem, point_send, point_recv, return_send, return_recv,
    heat_send, heat_recv, table_send, table_recv,
):
    dom, own = lax.axis_index("dom"), lax.axis_index("bin")
    doms, bins = lax.axis_size("dom"), lax.axis_size("bin")
    dom_up, dom_low = dom < doms - 1, dom > 0
    bin_up, bin_low = own < bins - 1, own > 0
    diag_up, diag_low = jnp.logical_and(dom_up, bin_up), jnp.logical_and(dom_low, bin_low)

    loads = []
    for z in range(ZT):
        z_at = pl.ds(z * 128, 128)
        loads.append((disp_in.at[:, :, :, z_at], disp.at[:, pl.ds(0, CX), z, pl.ds(8, CY), :]))
        loads.append((tile_in.at[:, :, z_at], tiles.at[:, z]))
        loads.append((moduli_in.at[:, :, :, z_at], moduli.at[:, :, z]))
        loads.append((mass_in.at[:, :, z_at], inverse.at[:, z]))
        loads.append((velo_in.at[:, :, :, z_at], velo.at[:, :, z]))
    loads = [pltpu.make_async_copy(a, b, in_sem.at[i]) for i, (a, b) in enumerate(loads)]
    for load in loads:
        load.start()

    disp[:, CX, :, :, :] = jnp.zeros((3, ZT, 32, 128), F32)
    col_in[...] = jnp.zeros_like(col_in)
    corner_in[...] = jnp.zeros_like(corner_in)
    layer_force_in[...] = jnp.zeros_like(layer_force_in)
    col_force_in[...] = jnp.zeros_like(col_force_in)
    corner_force_in[...] = jnp.zeros_like(corner_force_in)
    heat_in[...] = jnp.zeros_like(heat_in)
    for k in range(6):
        stress[k, 0] = jnp.zeros((ZT, CY, 128), F32)
        stress[k, CX + 1] = jnp.zeros((ZT, CY, 128), F32)
    for p in range(3):
        far[p, CX, :, 0:8, :] = jnp.zeros((ZT, 8, 128), F32)
        for i in range(NBIN):
            spread[i * (NBLK + 1) + NBLK, p] = jnp.full((8, 128), FAR, F32)
    met_own[NBLK] = jnp.zeros((2, 4, 8, 128), F32)
    met_over[NBLK] = jnp.zeros((2, 4, 8, 128), F32)
    heat_row[...] = jnp.zeros_like(heat_row)

    barrier = pltpu.get_barrier_semaphore()
    peers = [(dom, lax.rem(own + i, bins), None) for i in range(1, NBIN)]
    peers += [(dom + 1, own, dom_up), (dom - 1, own, dom_low)]
    peers += [(dom + 1, own + 1, diag_up), (dom - 1, own - 1, diag_low)]
    for to_dom, to_bin, exists in peers:
        def greet(to_dom=to_dom, to_bin=to_bin):
            pl.semaphore_signal(barrier, inc=1, device_id=(to_dom, to_bin), device_id_type=MESH)
        if exists is None:
            greet()
        else:
            pl.when(exists)(greet)

    def fill_slots(step, carry):
        named = [bins_ref[step, 0, b] for b in range(NBLK)]
        for b in range(NBLK):
            rank = jnp.int32(0)
            for before in range(b):
                rank = rank + (named[before] == named[b]).astype(I32)
            table[RANKS + step * NBLK + b] = rank & (CAP - 1)
            table[BINS + step * NBLK + b] = named[b]
        for k in range(NBIN):
            count = jnp.int32(0)
            found = [jnp.int32(NBLK)] * CAP
            for b in range(NBLK):
                same = named[b] == k
                for rank in range(CAP):
                    found[rank] = jnp.where(
                        jnp.logical_and(same, count == rank), jnp.int32(b), found[rank]
                    )
                count = count + same.astype(I32)
            for rank in range(CAP):
                table[(step * NBIN + k) * CAP + rank] = found[rank]
        return carry

    lax.fori_loop(0, SUB, fill_slots, 0)

    eye = lax.broadcasted_iota(I32, (SEG, SEG), 0) == lanes_of((SEG, SEG))

    def place_block(b, carry):
        node = node_ref[pl.ds(b, 1), :]
        x, y = lax.shift_right_logical(node, 13), lax.shift_right_logical(node, 9) & 15
        z = lax.shift_right_logical(node, 7) & 3
        row = (x * ZT + z) * CY + y
        lane = node & 127
        at = pl.ds(pl.multiple_of(b * SEG, SEG), SEG)
        row_ids = lax.broadcasted_iota(I32, (ROWS, SEG), 0)
        one_seg[:, at] = jnp.where(row_ids == row, 1.0, 0.0).astype(BF16)
        row_col = spread_row(row.astype(F32))
        ids = lanes_of((SEG, SEG)).astype(F32)
        for part in range(ROWS // 128):
            hits = jnp.where(row_col == ids + float(128 * part), 1.0, 0.0).astype(BF16)
            one_node[at, part * 128 : part * 128 + 128] = hits
        lane_col[at, :] = spread_row(lane.astype(F32))
        for c in range(3):
            base_col[c, at, :] = spread_row(base_ref[c : c + 1, at])
        heat_acc[at, :] = jnp.zeros((SEG, SEG), F32)
        return carry

    lax.fori_loop(0, NBLK, place_block, 0)

    for load in loads:
        load.wait()

    def scale(x, carry):
        for k in range(2):
            moduli[k, x] = moduli[k, x] * -0.0625
        inverse[x] = TIME_STEP / inverse[x]
        return carry

    lax.fori_loop(0, CX, scale, 0)

    greeted = jnp.int32(NBIN - 1)
    for _, _, exists in peers[NBIN - 1 :]:
        greeted = greeted + exists.astype(I32)
    pl.semaphore_wait(barrier, greeted)

    def remote(src, dst, index, to_dom, to_bin):
        return pltpu.make_async_remote_copy(
            src_ref=src, dst_ref=dst, send_sem=send_sem.at[index], recv_sem=recv_sem.at[index],
            device_id=(to_dom, to_bin), device_id_type=MESH,
        )

    def table_copy(i):
        return pltpu.make_async_remote_copy(
            src_ref=table, dst_ref=tables.at[i],
            send_sem=table_send.at[i], recv_sem=table_recv.at[i],
            device_id=(dom, lax.rem(own + bins - 1 - i, bins)), device_id_type=MESH,
        )

    for i in range(NBIN - 1):
        table_copy(i).start()
    inner = pl.ds(8, CY)
    layer_copy = remote(disp.at[:, 0, :, inner, :], disp.at[:, CX, :, inner, :], 0, dom - 1, own)
    col_copy = remote(col_out, col_in, 1, dom, own - 1)
    corner_copy = remote(corner_out, corner_in, 2, dom - 1, own - 1)
    layer_force_copy = remote(layer_force_out, layer_force_in, 3, dom + 1, own)
    col_force_copy = remote(col_force_out, col_force_in, 4, dom, own + 1)
    corner_force_copy = remote(corner_force_out, corner_force_in, 5, dom + 1, own + 1)

    def touching(step, slots_of, met, rows, alone):
        def with_block(b, carry):
            facing = slots_of(step, *mine_of(table, step, b))

            def with_rows(g, met_sums):
                met_sums = [list(each) for each in met_sums]
                at = pl.ds(pl.multiple_of(b * SEG + g * rows, rows), rows)
                wide = (rows // 8, 8, 128)
                mine = [seg_col[c, at, :].reshape(wide) for c in range(3)]
                if met is met_own:
                    sums = [jnp.zeros(wide, F32) for c in range(3)]
                else:
                    sums = [push_acc[c, at, :].reshape(wide) for c in range(3)]
                heat = heat_acc[at, :].reshape(wide)
                for j, slot in enumerate(facing):
                    delta = [mine[c] - spread[slot, c] for c in range(3)]
                    square = delta[0] * delta[0] + delta[1] * delta[1] + delta[2] * delta[2]
                    square = jnp.maximum(square, 1e-30)
                    over = lax.rsqrt(square)
                    pressure = jnp.maximum(RADIUS - square * over, 0.0)
                    weight = pressure * jnp.minimum(over, 1.0 / (0.25 * RADIUS))
                    parts = [weight * delta[c] for c in range(3)] + [pressure * pressure]
                    sums = [sums[c] + parts[c] for c in range(3)]
                    heat = heat + parts[3]
                    if j < alone:
                        continue
                    row = met_sums[j - alone]
                    for q in range(4):
                        row[q] = row[q] + jnp.sum(parts[q], axis=0)
                for c in range(3):
                    push_acc[c, at, :] = sums[c].reshape(rows, 128)
                heat_acc[at, :] = heat.reshape(rows, 128)
                return met_sums

            none = [[jnp.zeros((8, 128), F32)] * 4 for _ in facing[alone:]]
            met_sums = lax.fori_loop(0, SEG // rows, with_rows, none)
            for j, each in enumerate(met_sums):
                for q in range(4):
                    met[b, j, q] = each[q]
            return carry

        lax.fori_loop(0, NBLK, with_block, 0)

    high = (own >= NBIN // 2).astype(I32)

    def mine_of(numbers, step, b):
        return numbers[BINS + step * NBLK + b], numbers[RANKS + step * NBLK + b]

    def own_slots(step, named, rank):
        base = step * (NBIN * CAP) + named * CAP
        opposite = table[base + ((rank + 2) & (CAP - 1))]
        opposite = jnp.where(rank < CAP // 2, opposite, NBLK)
        return [table[base + rank], table[base + ((rank + 1) & (CAP - 1))], opposite]

    def next_slots(step, named, rank):
        base = step * (NBIN * CAP) + named * CAP
        ahead = [NEXT + tables[0, base + k] for k in range(CAP)]
        return ahead + [LAST + tables[2, base + k] for k in range(CAP)]

    def over_slots(step, named, rank):
        first = step * (NBIN * CAP) + named * CAP + ((rank + high) & 1)
        return [OVER + tables[1, first], OVER + tables[1, first + 2]]

    def rows_of(values):
        return jnp.sum(functools.reduce(lambda a, b: a + b, values), axis=0, keepdims=True)

    def substep(step, carry):
        parity = lax.rem(step, 2)

        for c in range(3):
            for z in range(ZT):
                corner_out[c * ZT + z : c * ZT + z + 1, :] = disp[c, 0, z, 8:9, :]
                for x in range(CX):
                    col_out[c, z, x : x + 1, :] = disp[c, x, z, 8:9, :]
        pl.when(dom_low)(layer_copy.start)
        pl.when(bin_low)(col_copy.start)
        pl.when(diag_low)(corner_copy.start)

        def split(pair, carry):
            for x in (2 * pair, 2 * pair + 1):
                at = pl.ds(pl.multiple_of(x * (ZT * CY), ZT * CY), ZT * CY)
                for c in range(3):
                    value = disp[c, x, :, 8 : 8 + CY, :].reshape(ZT * CY, 128)
                    for p, part in enumerate(pieces_of(value)):
                        split_disp[at, p * WIDE + c * 128 : p * WIDE + c * 128 + 128] = part
            return carry

        lax.fori_loop(0, CX // 2, split, 0)
        picked[...] = jnp.dot(one_node[...], split_disp[...], preferred_element_type=F32)

        def positions(pair, carry):
            for b in (2 * pair, 2 * pair + 1):
                at = pl.ds(pl.multiple_of(b * SEG, SEG), SEG)
                mask = lane_col[at, :] == lanes_of((SEG, SEG)).astype(F32)
                for c in range(3):
                    value = picked[at, c * 128 : c * 128 + 128]
                    value = value + picked[at, WIDE + c * 128 : WIDE + c * 128 + 128]
                    moved = jnp.where(mask, value, 0.0)
                    column = base_col[c, at, :] + jnp.sum(moved, axis=1, keepdims=True)
                    seg_col[c, at, :] = column
                    row = jnp.sum(jnp.where(eye, column, 0.0), axis=0, keepdims=True)
                    seg_row[c, pl.ds(b, 1), :] = row
                    spread[b, c] = jnp.broadcast_to(row, (8, 128))
            return carry

        lax.fori_loop(0, NBLK // 2, positions, 0)
        for i in range(NBIN - 1):
            point_copy(i, parity).start()

        touching(step, own_slots, met_own, ROWS_OWN, 1)

        def gather_own(b, carry):
            named, rank = mine_of(table, step, b)
            base = step * (NBIN * CAP) + named * CAP
            beside = table[base + ((rank + 3) & (CAP - 1))]
            opposite = table[base + ((rank + 2) & (CAP - 1))]
            opposite = jnp.where(rank >= CAP // 2, opposite, NBLK)
            for q in range(4):
                row = rows_of([met_own[beside, 0, q], met_own[opposite, 1, q]])
                own_rows[b, q : q + 1, :] = row
            return carry

        lax.fori_loop(0, NBLK, gather_own, 0)

        pl.when(dom_up)(layer_copy.wait_recv)
        pl.when(bin_up)(col_copy.wait_recv)
        pl.when(diag_up)(corner_copy.wait_recv)
        for c in range(3):
            for z in range(ZT):
                disp[c, CX, z, 24:25, :] = corner_in[c * ZT + z : c * ZT + z + 1, :]
                for x in range(CX):
                    disp[c, x, z, 24:25, :] = col_in[c, z, x : x + 1, :]

        def corners(part, carry):
            for x in [3 * part + i for i in range(3)]:
                for c in range(3):
                    low, high = disp[c, x, :, 8:24, :], disp[c, x, :, 9:25, :]
                    total, gap = low + high, high - low
                    total_next, gap_next = next_z(total), next_z(gap)
                    grads[c, 0, x] = total + total_next
                    grads[c, 1, x] = gap + gap_next
                    grads[c, 2, x] = total_next - total
            return carry

        lax.fori_loop(0, (CX + 1) // 3, corners, 0)

        def stresses(x, carry):
            g = [
                [grads[c, 0, x + 1] - grads[c, 0, x]]
                + [grads[c, q, x] + grads[c, q, x + 1] for q in (1, 2)]
                for c in range(3)
            ]
            lame, shear = moduli[0, x], moduli[1, x]
            volume = lame * (g[0][0] + g[1][1] + g[2][2])
            for p in range(3):
                stress[p, x + 1] = shear * (g[p][p] + g[p][p]) + volume
            stress[3, x + 1] = shear * (g[0][1] + g[1][0])
            stress[4, x + 1] = shear * (g[0][2] + g[2][0])
            stress[5, x + 1] = shear * (g[1][2] + g[2][1])
            return carry

        lax.fori_loop(0, CX, stresses, 0)

        def forces_on(x):
            for p, (kx, ky, kz) in enumerate(((0, 3, 4), (3, 1, 5), (4, 5, 2))):
                along_x = stress[kx, x] - stress[kx, x + 1]
                along_y = stress[ky, x] + stress[ky, x + 1]
                along_z = stress[kz, x] + stress[kz, x + 1]
                minus, plus = along_x - along_y, along_x + along_y
                near[p, x] = (minus - along_z) + last_z(minus + along_z)
                far[p, x, :, 8:24, :] = (plus - along_z) + last_z(plus + along_z)

        forces_on(CX)
        for p in range(3):
            layer_force_out[p] = near[p, CX] + far[p, CX, :, 7:23, :]
            for z in range(ZT):
                corner_force_out[p * ZT + z : p * ZT + z + 1, :] = far[p, CX, z, 23:24, :]
        pl.when(dom_up)(layer_force_copy.start)
        pl.when(diag_up)(corner_force_copy.start)

        def forces(pair, carry):
            for x in (2 * pair, 2 * pair + 1):
                forces_on(x)
            return carry

        lax.fori_loop(0, CX // 2, forces, 0)
        for p in range(3):
            for z in range(ZT):
                for x in range(CX):
                    col_force_out[p, z, x : x + 1, :] = far[p, x, z, 23:24, :]
        pl.when(bin_up)(col_force_copy.start)

        @pl.when(step == 0)
        def tables_here():
            for i in range(NBIN - 1):
                table_copy(i).wait()

        def spread_from(i):
            point_copy(i, parity).wait_recv()
            for b in range(NBLK):
                for c in range(3):
                    spread[NEXT * (i + 1) + b, c] = jnp.broadcast_to(
                        pool[parity, i, c, b : b + 1, :], (8, 128)
                    )

        spread_from(1)
        touching(step, over_slots, met_over, ROWS_OVER, 0)

        def gather_over(b, carry):
            named, rank = mine_of(tables.at[1], step, b)
            first = step * (NBIN * CAP) + named * CAP + ((rank + high) & 1)
            ones = [table[first], table[first + 2]]
            half = lax.shift_right_logical(rank, 1)
            for q in range(4):
                row = rows_of([met_over[one, half, q] for one in ones])
                return_out[b, q : q + 1, :] = row
            return carry

        lax.fori_loop(0, NBLK, gather_over, 0)
        return_copy.start()
        spread_from(0)
        spread_from(2)
        touching(step, next_slots, None, ROWS_NEXT, 2 * CAP)

        return_copy.wait_recv()

        def lay_push(pair, carry):
            for b in (2 * pair, 2 * pair + 1):
                at = pl.ds(pl.multiple_of(b * SEG, SEG), SEG)
                mask = lane_col[at, :] == lanes_of((SEG, SEG)).astype(F32)
                met = own_rows[b] + return_in[b]
                heat_row[b] = heat_row[b] + met[3:4, :]
                for c in range(3):
                    total = push_acc[c, at, :] - jnp.where(eye, met[c : c + 1, :], 0.0)
                    total = jnp.sum(total, axis=1, keepdims=True)
                    laid = jnp.where(mask, PENALTY * total, 0.0)
                    for p, part in enumerate(pieces_of(laid)):
                        split_push[at, p * WIDE + c * 128 : p * WIDE + c * 128 + 128] = part
            return carry

        lax.fori_loop(0, NBLK // 2, lay_push, 0)
        pushed[...] = jnp.dot(one_seg[...], split_push[...], preferred_element_type=F32)

        pl.when(dom_low)(layer_force_copy.wait_recv)
        pl.when(bin_low)(col_force_copy.wait_recv)
        pl.when(diag_low)(corner_force_copy.wait_recv)
        for p in range(3):
            near[p, 0] = near[p, 0] + layer_force_in[p]
            for z in range(ZT):
                near[p, 0, z, 0:1, :] = (
                    near[p, 0, z, 0:1, :] + corner_force_in[p * ZT + z : p * ZT + z + 1, :]
                )
                for x in range(CX):
                    far[p, x, z, 7:8, :] = col_force_in[p, z, x : x + 1, :]
        pl.when(dom_low)(layer_copy.wait_send)
        pl.when(bin_low)(col_copy.wait_send)
        pl.when(diag_low)(corner_copy.wait_send)
        pl.when(dom_up)(layer_force_copy.wait_send)
        pl.when(bin_up)(col_force_copy.wait_send)
        pl.when(diag_up)(corner_force_copy.wait_send)
        for i in range(NBIN - 1):
            point_copy(i, parity).wait_send()
        return_copy.wait_send()

        def advance(x, carry):
            for p in range(3):
                at = pl.ds(pl.multiple_of(x * (ZT * CY), ZT * CY), ZT * CY)
                force = near[p, x] + far[p, x, :, 7:23, :]
                for part in range(PIECES):
                    column = part * WIDE + p * 128
                    force = force + pushed[at, column : column + 128].reshape(ZT, CY, 128)
                moved = velo[p, x] + force * inverse[x]
                velo[p, x] = moved
                moved = disp[p, x, :, 8:24, :] + TIME_STEP * moved
                disp[p, x, :, 8:24, :] = moved
                disp_out[p, x] = moved
            return carry

        lax.fori_loop(0, CX, advance, 0)
        return carry

    def point_copy(i, parity):
        return pltpu.make_async_remote_copy(
            src_ref=seg_row, dst_ref=pool.at[parity, i],
            send_sem=point_send.at[i], recv_sem=point_recv.at[parity, i],
            device_id=(dom, lax.rem(own + bins - 1 - i, bins)), device_id_type=MESH,
        )

    return_copy = pltpu.make_async_remote_copy(
        src_ref=return_out, dst_ref=return_in, send_sem=return_send.at[0],
        recv_sem=return_recv.at[0], device_id=(dom, lax.rem(own + 2, bins)), device_id_type=MESH,
    )

    lax.fori_loop(0, SUB, substep, 0)

    device = dom * bins + own

    def split_tiles(x, carry):
        offset = tiles[x] - device * TILE_DEV + bins * TILE_DEV
        side = lax.shift_right_logical(offset, 10)
        row = side * 2 + (lax.shift_right_logical(offset, 7) & 1)
        at = pl.ds(pl.multiple_of(x * (ZT * CY), ZT * CY), ZT * CY)
        split_disp[at, 0:128] = row.astype(F32).astype(BF16).reshape(ZT * CY, 128)
        lane = (offset & 127).astype(F32).astype(BF16)
        split_disp[at, 128:256] = lane.reshape(ZT * CY, 128)
        return carry

    lax.fori_loop(0, CX, split_tiles, 0)

    def lay_heat(b, carry):
        at = pl.ds(pl.multiple_of(b * SEG, SEG), SEG)
        picked = jnp.dot(
            one_node[at, :], split_disp[:, 0:256], preferred_element_type=F32
        )
        ids = lanes_of((SEG, SEG)).astype(F32)
        mask = lane_col[at, :] == ids
        row_col = jnp.sum(jnp.where(mask, picked[:, 0:128], 0.0), axis=1, keepdims=True)
        lane = jnp.sum(jnp.where(mask, picked[:, 128:256], 0.0), axis=1, keepdims=True)
        tile_row[b, 0:1, :] = jnp.sum(jnp.where(eye, row_col, 0.0), axis=0, keepdims=True)
        total = heat_acc[at, :] + jnp.where(eye, heat_row[b], 0.0)
        total = SHORT_GAIN * jnp.sum(total, axis=1, keepdims=True)
        laid = jnp.where(lane == ids, total, 0.0)
        for p, part in enumerate(pieces_of(laid)):
            tile_lane[p, at, :] = part
        return carry

    lax.fori_loop(0, NBLK, lay_heat, 0)
    on_tiles = jnp.zeros((16, 128), F32)
    for b in range(NBLK):
        ids = lax.broadcasted_iota(I32, (16, SEG), 0).astype(F32)
        hits = jnp.where(ids == tile_row[b, 0:1, :], 1.0, 0.0).astype(BF16)
        for p in range(PIECES):
            on_tiles = on_tiles + jnp.dot(
                hits, tile_lane[p, b * SEG : (b + 1) * SEG, :], preferred_element_type=F32
            )
    for side in range(3):
        heat_parts[side, 0:2, :] = on_tiles[side * 2 : side * 2 + 2, :]

    def heat_copy(index, to_dom):
        return pltpu.make_async_remote_copy(
            src_ref=heat_parts.at[2 * index], dst_ref=heat_in.at[index],
            send_sem=heat_send.at[index], recv_sem=heat_recv.at[index],
            device_id=(to_dom, own), device_id_type=MESH,
        )

    to_low, to_up = heat_copy(0, dom - 1), heat_copy(1, dom + 1)
    pl.when(dom_low)(to_low.start)
    pl.when(dom_up)(to_up.start)
    pl.when(dom_up)(to_low.wait_recv)
    pl.when(dom_low)(to_up.wait_recv)
    heat_out[...] = heat_parts[1, 0:2, :] + heat_in[0, 0:2, :] + heat_in[1, 0:2, :]
    pl.when(dom_low)(to_low.wait_send)
    pl.when(dom_up)(to_up.wait_send)


def deliver(disp, velo, heat, disp_out, velo_out, heat_out, sem):
    stores = [(heat, heat_out)]
    for z in range(ZT):
        z_at = pl.ds(z * 128, 128)
        stores.append((disp.at[:, :, z], disp_out.at[:, :, :, z_at]))
        stores.append((velo.at[:, :, z], velo_out.at[:, :, :, z_at]))
    stores = [pltpu.make_async_copy(a, b, sem.at[i]) for i, (a, b) in enumerate(stores)]
    for store in stores:
        store.start()
    for store in stores:
        store.wait()


def per_device(displacement, velocity, moduli, nodal_mass, node, base, contact_bin, element_tile):
    anywhere = pl.BlockSpec(memory_space=pl.ANY)
    hbm = pl.BlockSpec(memory_space=pltpu.HBM)
    vmem = pl.BlockSpec(memory_space=pltpu.VMEM)
    smem = pl.BlockSpec(memory_space=pltpu.SMEM)
    dma, vec = pltpu.SemaphoreType.DMA, pltpu.VMEM
    slab = (ZT, CY, 128)
    scratch = [
        vec((3, CX + 1, ZT, 32, 128), F32),
        vec((2, CX) + slab, F32),
        vec((CX,) + slab, F32),
        vec((CX,) + slab, I32),
        vec((ROWS, NSEG), BF16),
        vec((NSEG, ROWS), BF16),
        vec((NSEG, 128), F32),
        vec((3, NSEG, 128), F32),
        vec((PIECES, NSEG, 128), BF16),
        vec((NBLK, 8, 128), F32),
        vec((ROWS, PIECES * WIDE), BF16),
        vec((NSEG, PIECES * WIDE), BF16),
        vec((3, NSEG, 128), F32),
        vec((3, NBLK, 128), F32),
        vec((2, NBIN - 1, 3, NBLK, 128), F32),
        vec((NBIN * (NBLK + 1), 3, 8, 128), F32),
        vec((NBLK + 1, 2, 4, 8, 128), F32),
        vec((NBLK + 1, 2, 4, 8, 128), F32),
        vec((NBLK, 4, 128), F32),
        vec((NBLK, 4, 128), F32),
        vec((NBLK, 4, 128), F32),
        vec((NBLK, 1, 128), F32),
        vec((3, NSEG, 128), F32),
        vec((NSEG, 128), F32),
        vec((NSEG, PIECES * WIDE), F32),
        vec((ROWS, PIECES * WIDE), F32),
        vec((3, 3, CX + 1) + slab, F32),
        vec((6, CX + 2) + slab, F32),
        vec((3, CX + 1) + slab, F32),
        vec((3, CX + 1, ZT, 32, 128), F32),
        vec((3, ZT, CX, 128), F32),
        vec((3, ZT, CX, 128), F32),
        vec((16, 128), F32),
        vec((16, 128), F32),
        vec((3,) + slab, F32),
        vec((3,) + slab, F32),
        vec((3, ZT, CX, 128), F32),
        vec((3, ZT, CX, 128), F32),
        vec((16, 128), F32),
        vec((16, 128), F32),
        vec((3, 8, 128), F32),
        vec((2, 8, 128), F32),
        pltpu.SMEM((TABLE,), I32),
        pltpu.SMEM((NBIN - 1, TABLE), I32),
        dma((5 * ZT,)),
        dma((6,)),
        dma((6,)),
        dma((NBIN - 1,)),
        dma((2, NBIN - 1)),
        dma((1,)),
        dma((1,)),
        dma((2,)),
        dma((2,)),
        dma((NBIN - 1,)),
        dma((NBIN - 1,)),
    ]
    results = pl.pallas_call(
        kernel,
        out_shape=(
            pltpu.VMEM((3, CX) + slab, F32),
            pltpu.VMEM((3, CX) + slab, F32),
            pltpu.VMEM((2, 128), F32),
        ),
        in_specs=[hbm] * 5 + [vmem, vmem, smem],
        out_specs=(vmem, vmem, vmem),
        scratch_shapes=scratch,
        compiler_params=pltpu.CompilerParams(
            collective_id=0, has_side_effects=True, vmem_limit_bytes=65339392
        ),
        name="module_substeps",
    )(
        displacement, velocity, moduli, nodal_mass, element_tile,
        node.reshape(NBLK, SEG), base, contact_bin.transpose(0, 2, 1),
    )
    new_displacement, new_velocity, heat = pl.pallas_call(
        deliver,
        out_shape=(
            jax.ShapeDtypeStruct(displacement.shape, F32),
            jax.ShapeDtypeStruct(velocity.shape, F32),
            jax.ShapeDtypeStruct((2, 128), F32),
        ),
        in_specs=[vmem] * 3,
        out_specs=(hbm, hbm, hbm),
        scratch_shapes=[dma((2 * ZT + 1,))],
        name="deliver",
    )(*[pltpu.with_memory_space_constraint(x, pltpu.VMEM) for x in results])
    return new_displacement, new_velocity, heat.reshape(-1)


def solution(mesh):
    placed = (
        P(None, "dom", "bin", None),
        P(None, "dom", "bin", None),
        P(None, "dom", "bin", None),
        P("dom", "bin", None),
        P(("dom", "bin")),
        P(None, ("dom", "bin")),
        P(None, ("dom", "bin"), None),
        P("dom", "bin", None),
    )
    return jax.shard_map(
        per_device,
        mesh=mesh,
        in_specs=placed,
        out_specs=(P(None, "dom", "bin", None), P(None, "dom", "bin", None), P(("dom", "bin"))),
        check_vma=False,
    )
```

```python
import functools

import jax
import jax.numpy as jnp
from jax import lax
from jax.experimental import pallas as pl
from jax.experimental.pallas import tpu as pltpu
from jax.sharding import PartitionSpec as P

SUB = 4
SEG = 128
TILE_DEV = 256
RADIUS = 0.09
PENALTY = 4.0
SHORT_GAIN = 100.0
TIME_STEP = 0.2

CX, CY, ZT = 8, 16, 4
NBLK, CAP, NBIN = 8, 4, 4
NSEG = NBLK * SEG
ROWS = CX * ZT * CY
PIECES = 2
ROWS_OWN, ROWS_OVER, ROWS_NEXT = 64, 64, 64
WIDE = 384
FAR = 1e12
BINS = SUB * NBIN * CAP
RANKS = BINS + SUB * NBLK
TABLE = RANKS + SUB * NBLK
NEXT, OVER, LAST = NBLK + 1, 2 * (NBLK + 1), 3 * (NBLK + 1)
MESH = pl.DeviceIdType.MESH
F32, BF16, I32 = jnp.float32, jnp.bfloat16, jnp.int32


def pieces_of(value):
    parts = []
    for _ in range(PIECES):
        part = value.astype(BF16)
        parts.append(part)
        value = value - part.astype(F32)
    return parts


def lanes_of(shape):
    return lax.broadcasted_iota(I32, shape, len(shape) - 1)


def next_z(value):
    turned = pltpu.roll(value, 127, 2)
    beyond = jnp.concatenate([turned[1:], turned[:1]], axis=0)
    return jnp.where(lanes_of(value.shape) == 127, beyond, turned)


def last_z(value):
    turned = pltpu.roll(value, 1, 2)
    before = jnp.concatenate([turned[-1:], turned[:-1]], axis=0)
    return jnp.where(lanes_of(value.shape) == 0, before, turned)


def spread_row(row):
    return jnp.broadcast_to(row, (SEG, SEG)).T


def kernel(
    disp_in, velo_in, moduli_in, mass_in, tile_in, node_ref, base_ref, bins_ref,
    disp_out, velo, heat_out,
    disp, moduli, inverse, tiles,
    one_seg, one_node, lane_col, base_col, tile_lane, tile_row, tile_col,
    split_disp, split_push, seg_col, seg_row, pool, spread,
    met_own, met_over, own_rows, return_out, return_in, heat_row,
    push_acc, heat_acc, picked, pushed,
    grads, stress, near, far,
    col_out, col_in, corner_out, corner_in,
    edge, turned, layer_force_in, col_force_out, col_force_in,
    corner_force_out, corner_force_in,
    heat_parts, heat_in, table, tables,
    in_sem, send_sem, recv_sem, point_send, point_recv, return_send, return_recv,
    heat_send, heat_recv, table_send, table_recv,
):
    dom, own = lax.axis_index("dom"), lax.axis_index("bin")
    doms, bins = lax.axis_size("dom"), lax.axis_size("bin")
    dom_up, dom_low = dom < doms - 1, dom > 0
    bin_up, bin_low = own < bins - 1, own > 0
    diag_up, diag_low = jnp.logical_and(dom_up, bin_up), jnp.logical_and(dom_low, bin_low)

    loads = []
    for z in range(ZT):
        z_at = pl.ds(z * 128, 128)
        loads.append((disp_in.at[:, :, :, z_at], disp.at[:, pl.ds(0, CX), z, pl.ds(8, CY), :]))
        loads.append((tile_in.at[:, :, z_at], tiles.at[:, z]))
        loads.append((moduli_in.at[:, :, :, z_at], moduli.at[:, :, z]))
        loads.append((mass_in.at[:, :, z_at], inverse.at[:, z]))
        loads.append((velo_in.at[:, :, :, z_at], velo.at[:, :, z]))
    loads = [pltpu.make_async_copy(a, b, in_sem.at[i]) for i, (a, b) in enumerate(loads)]
    for load in loads:
        load.start()

    disp[:, CX, :, :, :] = jnp.zeros((3, ZT, 32, 128), F32)
    col_in[...] = jnp.zeros_like(col_in)
    corner_in[...] = jnp.zeros_like(corner_in)
    layer_force_in[...] = jnp.zeros_like(layer_force_in)
    col_force_in[...] = jnp.zeros_like(col_force_in)
    corner_force_in[...] = jnp.zeros_like(corner_force_in)
    heat_in[...] = jnp.zeros_like(heat_in)
    for k in range(6):
        stress[k, 0] = jnp.zeros((ZT, CY, 128), F32)
        stress[k, CX + 1] = jnp.zeros((ZT, CY, 128), F32)
    for p in range(3):
        for k in range(2):
            for x in range(CX + 1):
                far[k, p, x, :, 0:8, :] = jnp.zeros((ZT, 8, 128), F32)
        for i in range(NBIN):
            spread[i * (NBLK + 1) + NBLK, p] = jnp.full((8, 128), FAR, F32)
    met_own[NBLK] = jnp.zeros((2, 4, 8, 128), F32)
    met_over[NBLK] = jnp.zeros((2, 4, 8, 128), F32)
    heat_row[...] = jnp.zeros_like(heat_row)

    barrier = pltpu.get_barrier_semaphore()
    peers = [(dom, lax.rem(own + i, bins), None) for i in range(1, NBIN)]
    peers += [(dom + 1, own, dom_up), (dom - 1, own, dom_low)]
    peers += [(dom + 1, own + 1, diag_up), (dom - 1, own - 1, diag_low)]
    for to_dom, to_bin, exists in peers:
        def greet(to_dom=to_dom, to_bin=to_bin):
            pl.semaphore_signal(barrier, inc=1, device_id=(to_dom, to_bin), device_id_type=MESH)
        if exists is None:
            greet()
        else:
            pl.when(exists)(greet)

    def fill_slots(step, carry):
        named = [bins_ref[step, 0, b] for b in range(NBLK)]
        for b in range(NBLK):
            rank = jnp.int32(0)
            for before in range(b):
                rank = rank + (named[before] == named[b]).astype(I32)
            table[RANKS + step * NBLK + b] = rank & (CAP - 1)
            table[BINS + step * NBLK + b] = named[b]
        for k in range(NBIN):
            count = jnp.int32(0)
            found = [jnp.int32(NBLK)] * CAP
            for b in range(NBLK):
                same = named[b] == k
                for rank in range(CAP):
                    found[rank] = jnp.where(
                        jnp.logical_and(same, count == rank), jnp.int32(b), found[rank]
                    )
                count = count + same.astype(I32)
            for rank in range(CAP):
                table[(step * NBIN + k) * CAP + rank] = found[rank]
        return carry

    lax.fori_loop(0, SUB, fill_slots, 0)

    eye = lax.broadcasted_iota(I32, (SEG, SEG), 0) == lanes_of((SEG, SEG))

    def place_block(b, carry):
        node = node_ref[pl.ds(b, 1), :]
        x, y = lax.shift_right_logical(node, 13), lax.shift_right_logical(node, 9) & 15
        z = lax.shift_right_logical(node, 7) & 3
        row = (x * ZT + z) * CY + y
        lane = node & 127
        at = pl.ds(pl.multiple_of(b * SEG, SEG), SEG)
        row_ids = lax.broadcasted_iota(I32, (ROWS, SEG), 0)
        one_seg[:, at] = jnp.where(row_ids == row, 1.0, 0.0).astype(BF16)
        row_col = spread_row(row.astype(F32))
        ids = lanes_of((SEG, SEG)).astype(F32)
        for part in range(ROWS // 128):
            hits = jnp.where(row_col == ids + float(128 * part), 1.0, 0.0).astype(BF16)
            one_node[at, part * 128 : part * 128 + 128] = hits
        lane_col[at, :] = spread_row(lane.astype(F32))
        for c in range(3):
            base_col[c, at, :] = spread_row(base_ref[c : c + 1, at])
        heat_acc[at, :] = jnp.zeros((SEG, SEG), F32)
        return carry

    lax.fori_loop(0, NBLK, place_block, 0)

    for load in loads:
        load.wait()

    def scale(x, carry):
        for k in range(2):
            moduli[k, x] = moduli[k, x] * -0.0625
        inverse[x] = TIME_STEP / inverse[x]
        return carry

    lax.fori_loop(0, CX, scale, 0)

    device = dom * bins + own

    def split_tiles(x, carry):
        offset = tiles[x] - device * TILE_DEV + bins * TILE_DEV
        side = lax.shift_right_logical(offset, 10)
        row = side * 2 + (lax.shift_right_logical(offset, 7) & 1)
        at = pl.ds(pl.multiple_of(x * (ZT * CY), ZT * CY), ZT * CY)
        split_disp[at, 0:128] = row.astype(F32).astype(BF16).reshape(ZT * CY, 128)
        lane = (offset & 127).astype(F32).astype(BF16)
        split_disp[at, 128:256] = lane.reshape(ZT * CY, 128)
        return carry

    lax.fori_loop(0, CX, split_tiles, 0)
    picked[:, 0:256] = jnp.dot(
        one_node[...], split_disp[:, 0:256], preferred_element_type=F32
    )

    def place_tiles(b, carry):
        at = pl.ds(pl.multiple_of(b * SEG, SEG), SEG)
        ids = lanes_of((SEG, SEG)).astype(F32)
        mask = lane_col[at, :] == ids
        row_col = jnp.sum(jnp.where(mask, picked[at, 0:128], 0.0), axis=1, keepdims=True)
        lane = jnp.sum(jnp.where(mask, picked[at, 128:256], 0.0), axis=1, keepdims=True)
        tile_col[at, :] = jnp.broadcast_to(lane, (SEG, SEG))
        row = jnp.sum(jnp.where(eye, row_col, 0.0), axis=0, keepdims=True)
        ids = lax.broadcasted_iota(I32, (16, SEG), 0).astype(F32)
        tile_row[:, at] = jnp.where(ids == row, 1.0, 0.0).astype(BF16)
        return carry

    lax.fori_loop(0, NBLK, place_tiles, 0)

    greeted = jnp.int32(NBIN - 1)
    for _, _, exists in peers[NBIN - 1 :]:
        greeted = greeted + exists.astype(I32)
    pl.semaphore_wait(barrier, greeted)

    def remote(src, dst, index, to_dom, to_bin):
        return pltpu.make_async_remote_copy(
            src_ref=src, dst_ref=dst, send_sem=send_sem.at[index], recv_sem=recv_sem.at[index],
            device_id=(to_dom, to_bin), device_id_type=MESH,
        )

    def table_copy(i):
        return pltpu.make_async_remote_copy(
            src_ref=table, dst_ref=tables.at[i],
            send_sem=table_send.at[i], recv_sem=table_recv.at[i],
            device_id=(dom, lax.rem(own + bins - 1 - i, bins)), device_id_type=MESH,
        )

    for i in range(NBIN - 1):
        table_copy(i).start()
    inner = pl.ds(8, CY)
    layer_copy = remote(disp.at[:, 0, :, inner, :], disp.at[:, CX, :, inner, :], 0, dom - 1, own)
    col_copy = remote(col_out, col_in, 1, dom, own - 1)
    corner_copy = remote(corner_out, corner_in, 2, dom - 1, own - 1)
    layer_force_copy = remote(near.at[:, CX], layer_force_in, 3, dom + 1, own)
    col_force_copy = remote(col_force_out, col_force_in, 4, dom, own + 1)
    corner_force_copy = remote(corner_force_out, corner_force_in, 5, dom + 1, own + 1)

    def touching(step, slots_of, met, rows, alone):
        def with_block(b, carry):
            facing = slots_of(step, *mine_of(table, step, b))

            def with_rows(g, met_sums):
                met_sums = [list(each) for each in met_sums]
                at = pl.ds(pl.multiple_of(b * SEG + g * rows, rows), rows)
                wide = (rows // 8, 8, 128)
                mine = [seg_col[c, at, :].reshape(wide) for c in range(3)]
                if met is met_own:
                    sums = [jnp.zeros(wide, F32) for c in range(3)]
                else:
                    sums = [push_acc[c, at, :].reshape(wide) for c in range(3)]
                heat = heat_acc[at, :].reshape(wide)
                for j, slot in enumerate(facing):
                    delta = [mine[c] - spread[slot, c] for c in range(3)]
                    square = delta[0] * delta[0] + delta[1] * delta[1] + delta[2] * delta[2]
                    square = jnp.maximum(square, 1e-30)
                    over = lax.rsqrt(square)
                    pressure = jnp.maximum(RADIUS - square * over, 0.0)
                    weight = pressure * jnp.minimum(over, 1.0 / (0.25 * RADIUS))
                    parts = [weight * delta[c] for c in range(3)] + [pressure * pressure]
                    sums = [sums[c] + parts[c] for c in range(3)]
                    heat = heat + parts[3]
                    if j < alone:
                        continue
                    row = met_sums[j - alone]
                    for q in range(4):
                        row[q] = row[q] + jnp.sum(parts[q], axis=0)
                for c in range(3):
                    push_acc[c, at, :] = sums[c].reshape(rows, 128)
                heat_acc[at, :] = heat.reshape(rows, 128)
                return met_sums

            none = [[jnp.zeros((8, 128), F32)] * 4 for _ in facing[alone:]]
            met_sums = lax.fori_loop(0, SEG // rows, with_rows, none)
            for j, each in enumerate(met_sums):
                for q in range(4):
                    met[b, j, q] = each[q]
            return carry

        lax.fori_loop(0, NBLK, with_block, 0)

    high = (own >= NBIN // 2).astype(I32)

    def mine_of(numbers, step, b):
        return numbers[BINS + step * NBLK + b], numbers[RANKS + step * NBLK + b]

    def own_slots(step, named, rank):
        base = step * (NBIN * CAP) + named * CAP
        opposite = table[base + ((rank + 2) & (CAP - 1))]
        opposite = jnp.where(rank < CAP // 2, opposite, NBLK)
        return [table[base + rank], table[base + ((rank + 1) & (CAP - 1))], opposite]

    def next_slots(step, named, rank):
        base = step * (NBIN * CAP) + named * CAP
        ahead = [NEXT + tables[0, base + k] for k in range(CAP)]
        return ahead + [LAST + tables[2, base + k] for k in range(CAP)]

    def over_slots(step, named, rank):
        first = step * (NBIN * CAP) + named * CAP + ((rank + high) & 1)
        return [OVER + tables[1, first], OVER + tables[1, first + 2]]

    def rows_of(values):
        return jnp.sum(functools.reduce(lambda a, b: a + b, values), axis=0, keepdims=True)

    def heat_copy(index, to_dom):
        return pltpu.make_async_remote_copy(
            src_ref=heat_parts.at[2 * index], dst_ref=heat_in.at[index],
            send_sem=heat_send.at[index], recv_sem=heat_recv.at[index],
            device_id=(to_dom, own), device_id_type=MESH,
        )

    to_low, to_up = heat_copy(0, dom - 1), heat_copy(1, dom + 1)

    def send_heat():
        def lay_heat(b, carry):
            at = pl.ds(pl.multiple_of(b * SEG, SEG), SEG)
            met = heat_row[b] + own_rows[b, 3:4, :] + return_in[b, 3:4, :]
            total = heat_acc[at, :] + jnp.where(eye, met, 0.0)
            total = SHORT_GAIN * jnp.sum(total, axis=1, keepdims=True)
            laid = jnp.where(tile_col[at, :] == lanes_of((SEG, SEG)).astype(F32), total, 0.0)
            for p, part in enumerate(pieces_of(laid)):
                tile_lane[at, p * 128 : p * 128 + 128] = part
            return carry

        lax.fori_loop(0, NBLK, lay_heat, 0)
        laid = jnp.dot(tile_row[...], tile_lane[...], preferred_element_type=F32)
        on_tiles = laid[:, 0:128] + laid[:, 128:256]
        for side in range(3):
            heat_parts[side, 0:2, :] = on_tiles[side * 2 : side * 2 + 2, :]
        pl.when(dom_low)(to_low.start)
        pl.when(dom_up)(to_up.start)

    def substep(step, carry):
        parity = lax.rem(step, 2)

        for c in range(3):
            for z in range(ZT):
                corner_out[c * ZT + z : c * ZT + z + 1, :] = disp[c, 0, z, 8:9, :]
                for x in range(CX):
                    col_out[c, z, x : x + 1, :] = disp[c, x, z, 8:9, :]
        pl.when(dom_low)(layer_copy.start)
        pl.when(bin_low)(col_copy.start)
        pl.when(diag_low)(corner_copy.start)

        def split(pair, carry):
            for x in (2 * pair, 2 * pair + 1):
                at = pl.ds(pl.multiple_of(x * (ZT * CY), ZT * CY), ZT * CY)
                for c in range(3):
                    value = disp[c, x, :, 8 : 8 + CY, :].reshape(ZT * CY, 128)
                    for p, part in enumerate(pieces_of(value)):
                        split_disp[at, p * WIDE + c * 128 : p * WIDE + c * 128 + 128] = part
            return carry

        lax.fori_loop(0, CX // 2, split, 0)
        picked[...] = jnp.dot(one_node[...], split_disp[...], preferred_element_type=F32)

        def positions(pair, carry):
            for b in (2 * pair, 2 * pair + 1):
                at = pl.ds(pl.multiple_of(b * SEG, SEG), SEG)
                mask = lane_col[at, :] == lanes_of((SEG, SEG)).astype(F32)
                for c in range(3):
                    value = picked[at, c * 128 : c * 128 + 128]
                    value = value + picked[at, WIDE + c * 128 : WIDE + c * 128 + 128]
                    moved = jnp.where(mask, value, 0.0)
                    column = base_col[c, at, :] + jnp.sum(moved, axis=1, keepdims=True)
                    seg_col[c, at, :] = column
                    row = jnp.sum(jnp.where(eye, column, 0.0), axis=0, keepdims=True)
                    seg_row[c, pl.ds(b, 1), :] = row
                    spread[b, c] = jnp.broadcast_to(row, (8, 128))
            return carry

        lax.fori_loop(0, NBLK // 2, positions, 0)
        for i in range(NBIN - 1):
            point_copy(i, parity).start()

        touching(step, own_slots, met_own, ROWS_OWN, 1)

        def gather_own(b, carry):
            named, rank = mine_of(table, step, b)
            base = step * (NBIN * CAP) + named * CAP
            beside = table[base + ((rank + 3) & (CAP - 1))]
            opposite = table[base + ((rank + 2) & (CAP - 1))]
            opposite = jnp.where(rank >= CAP // 2, opposite, NBLK)
            for q in range(4):
                row = rows_of([met_own[beside, 0, q], met_own[opposite, 1, q]])
                own_rows[b, q : q + 1, :] = row
            return carry

        lax.fori_loop(0, NBLK, gather_own, 0)

        pl.when(dom_up)(layer_copy.wait_recv)
        pl.when(bin_up)(col_copy.wait_recv)
        pl.when(diag_up)(corner_copy.wait_recv)
        for c in range(3):
            for z in range(ZT):
                disp[c, CX, z, 24:25, :] = corner_in[c * ZT + z : c * ZT + z + 1, :]
                for x in range(CX):
                    disp[c, x, z, 24:25, :] = col_in[c, z, x : x + 1, :]
            edge[...] = next_z(col_in[c])
            for z in range(ZT):
                for x in range(CX):
                    turned[c, x, z, 24:25, :] = edge[z, x : x + 1, :]
            turned[c, CX, :, 24:32, :] = next_z(disp[c, CX, :, 24:32, :])

        def corners(part, carry):
            for x in [3 * part + i for i in range(3)]:
                for c in range(3):
                    low, high = disp[c, x, :, 8:24, :], disp[c, x, :, 9:25, :]
                    low_next = next_z(low)
                    turned[c, x, :, 8:24, :] = low_next
                    high_next = turned[c, x, :, 9:25, :]
                    at_low, at_high = low + low_next, high + high_next
                    grads[c, 0, x] = at_low + at_high
                    grads[c, 1, x] = at_high - at_low
                    grads[c, 2, x] = (low_next - low) + (high_next - high)
            return carry

        lax.fori_loop(0, (CX + 1) // 3, corners, 0)

        def stresses(x, carry):
            g = [
                [grads[c, 0, x + 1] - grads[c, 0, x]]
                + [grads[c, q, x] + grads[c, q, x + 1] for q in (1, 2)]
                for c in range(3)
            ]
            lame, shear = moduli[0, x], moduli[1, x]
            volume = lame * (g[0][0] + g[1][1] + g[2][2])
            for p in range(3):
                stress[p, x + 1] = shear * (g[p][p] + g[p][p]) + volume
            stress[3, x + 1] = shear * (g[0][1] + g[1][0])
            stress[4, x + 1] = shear * (g[0][2] + g[2][0])
            stress[5, x + 1] = shear * (g[1][2] + g[2][1])
            return carry

        lax.fori_loop(0, CX, stresses, 0)

        def forces_on(x):
            for p, (kx, ky, kz) in enumerate(((0, 3, 4), (3, 1, 5), (4, 5, 2))):
                along_x = stress[kx, x] - stress[kx, x + 1]
                along_y = stress[ky, x] + stress[ky, x + 1]
                along_z = stress[kz, x] + stress[kz, x + 1]
                minus, plus = along_x - along_y, along_x + along_y
                far[0, p, x, :, 8:24, :] = plus - along_z
                far[1, p, x, :, 8:24, :] = plus + along_z
                here = minus - along_z + far[0, p, x, :, 7:23, :]
                near[p, x] = here + last_z(minus + along_z + far[1, p, x, :, 7:23, :])

        forces_on(CX)
        for p in range(3):
            ends = far[0, p, CX, :, 16:24, :] + last_z(far[1, p, CX, :, 16:24, :])
            for z in range(ZT):
                corner_force_out[p * ZT + z : p * ZT + z + 1, :] = ends[z, 7:8, :]
        pl.when(dom_up)(layer_force_copy.start)
        pl.when(diag_up)(corner_force_copy.start)

        def forces(pair, carry):
            for x in (2 * pair, 2 * pair + 1):
                forces_on(x)
            return carry

        lax.fori_loop(0, CX // 2, forces, 0)
        for p in range(3):
            for z in range(ZT):
                for x in range(CX):
                    col_force_out[p, z, x : x + 1, :] = far[0, p, x, z, 23:24, :]
                    edge[z, x : x + 1, :] = far[1, p, x, z, 23:24, :]
            col_force_out[p] = col_force_out[p] + last_z(edge[...])
        pl.when(bin_up)(col_force_copy.start)

        @pl.when(step == 0)
        def tables_here():
            for i in range(NBIN - 1):
                table_copy(i).wait()

        def spread_from(i):
            point_copy(i, parity).wait_recv()
            for b in range(NBLK):
                for c in range(3):
                    spread[NEXT * (i + 1) + b, c] = jnp.broadcast_to(
                        pool[parity, i, c, b : b + 1, :], (8, 128)
                    )

        spread_from(1)
        touching(step, over_slots, met_over, ROWS_OVER, 0)

        def gather_over(b, carry):
            named, rank = mine_of(tables.at[1], step, b)
            first = step * (NBIN * CAP) + named * CAP + ((rank + high) & 1)
            ones = [table[first], table[first + 2]]
            half = lax.shift_right_logical(rank, 1)
            for q in range(4):
                row = rows_of([met_over[one, half, q] for one in ones])
                return_out[b, q : q + 1, :] = row
            return carry

        lax.fori_loop(0, NBLK, gather_over, 0)
        return_copy.start()
        spread_from(0)
        spread_from(2)
        touching(step, next_slots, None, ROWS_NEXT, 2 * CAP)

        return_copy.wait_recv()
        pl.when(step == SUB - 1)(send_heat)


        def lay_push(pair, carry):
            for b in (2 * pair, 2 * pair + 1):
                at = pl.ds(pl.multiple_of(b * SEG, SEG), SEG)
                mask = lane_col[at, :] == lanes_of((SEG, SEG)).astype(F32)
                met = own_rows[b] + return_in[b]
                heat_row[b] = heat_row[b] + met[3:4, :]
                for c in range(3):
                    total = push_acc[c, at, :] - jnp.where(eye, met[c : c + 1, :], 0.0)
                    total = jnp.sum(total, axis=1, keepdims=True)
                    laid = jnp.where(mask, PENALTY * total, 0.0)
                    for p, part in enumerate(pieces_of(laid)):
                        split_push[at, p * WIDE + c * 128 : p * WIDE + c * 128 + 128] = part
            return carry

        lax.fori_loop(0, NBLK // 2, lay_push, 0)
        pushed[...] = jnp.dot(one_seg[...], split_push[...], preferred_element_type=F32)

        pl.when(dom_low)(layer_force_copy.wait_recv)
        pl.when(bin_low)(col_force_copy.wait_recv)
        pl.when(diag_low)(corner_force_copy.wait_recv)
        for p in range(3):
            near[p, 0] = near[p, 0] + layer_force_in[p]
            for z in range(ZT):
                near[p, 0, z, 0:1, :] = (
                    near[p, 0, z, 0:1, :] + corner_force_in[p * ZT + z : p * ZT + z + 1, :]
                )
                for x in range(CX):
                    near[p, x, z, 0:1, :] = (
                        near[p, x, z, 0:1, :] + col_force_in[p, z, x : x + 1, :]
                    )
        pl.when(dom_low)(layer_copy.wait_send)
        pl.when(bin_low)(col_copy.wait_send)
        pl.when(diag_low)(corner_copy.wait_send)
        pl.when(dom_up)(layer_force_copy.wait_send)
        pl.when(bin_up)(col_force_copy.wait_send)
        pl.when(diag_up)(corner_force_copy.wait_send)
        for i in range(NBIN - 1):
            point_copy(i, parity).wait_send()
        return_copy.wait_send()

        def advance(x, carry):
            for p in range(3):
                at = pl.ds(pl.multiple_of(x * (ZT * CY), ZT * CY), ZT * CY)
                force = near[p, x]
                for part in range(PIECES):
                    column = part * WIDE + p * 128
                    force = force + pushed[at, column : column + 128].reshape(ZT, CY, 128)
                moved = velo[p, x] + force * inverse[x]
                velo[p, x] = moved
                moved = disp[p, x, :, 8:24, :] + TIME_STEP * moved
                disp[p, x, :, 8:24, :] = moved
                disp_out[p, x] = moved
            return carry

        lax.fori_loop(0, CX, advance, 0)
        return carry

    def point_copy(i, parity):
        return pltpu.make_async_remote_copy(
            src_ref=seg_row, dst_ref=pool.at[parity, i],
            send_sem=point_send.at[i], recv_sem=point_recv.at[parity, i],
            device_id=(dom, lax.rem(own + bins - 1 - i, bins)), device_id_type=MESH,
        )

    return_copy = pltpu.make_async_remote_copy(
        src_ref=return_out, dst_ref=return_in, send_sem=return_send.at[0],
        recv_sem=return_recv.at[0], device_id=(dom, lax.rem(own + 2, bins)), device_id_type=MESH,
    )

    lax.fori_loop(0, SUB, substep, 0)

    pl.when(dom_up)(to_low.wait_recv)
    pl.when(dom_low)(to_up.wait_recv)
    heat_out[...] = heat_parts[1, 0:2, :] + heat_in[0, 0:2, :] + heat_in[1, 0:2, :]
    pl.when(dom_low)(to_low.wait_send)
    pl.when(dom_up)(to_up.wait_send)


def deliver(disp, velo, heat, disp_out, velo_out, heat_out, sem):
    stores = [(heat, heat_out)]
    for z in range(ZT):
        z_at = pl.ds(z * 128, 128)
        stores.append((disp.at[:, :, z], disp_out.at[:, :, :, z_at]))
        stores.append((velo.at[:, :, z], velo_out.at[:, :, :, z_at]))
    stores = [pltpu.make_async_copy(a, b, sem.at[i]) for i, (a, b) in enumerate(stores)]
    for store in stores:
        store.start()
    for store in stores:
        store.wait()


def per_device(displacement, velocity, moduli, nodal_mass, node, base, contact_bin, element_tile):
    anywhere = pl.BlockSpec(memory_space=pl.ANY)
    hbm = pl.BlockSpec(memory_space=pltpu.HBM)
    vmem = pl.BlockSpec(memory_space=pltpu.VMEM)
    smem = pl.BlockSpec(memory_space=pltpu.SMEM)
    dma, vec = pltpu.SemaphoreType.DMA, pltpu.VMEM
    slab = (ZT, CY, 128)
    scratch = [
        vec((3, CX + 1, ZT, 32, 128), F32),
        vec((2, CX) + slab, F32),
        vec((CX,) + slab, F32),
        vec((CX,) + slab, I32),
        vec((ROWS, NSEG), BF16),
        vec((NSEG, ROWS), BF16),
        vec((NSEG, 128), F32),
        vec((3, NSEG, 128), F32),
        vec((NSEG, PIECES * 128), BF16),
        vec((16, NSEG), BF16),
        vec((NSEG, 128), F32),
        vec((ROWS, PIECES * WIDE), BF16),
        vec((NSEG, PIECES * WIDE), BF16),
        vec((3, NSEG, 128), F32),
        vec((3, NBLK, 128), F32),
        vec((2, NBIN - 1, 3, NBLK, 128), F32),
        vec((NBIN * (NBLK + 1), 3, 8, 128), F32),
        vec((NBLK + 1, 2, 4, 8, 128), F32),
        vec((NBLK + 1, 2, 4, 8, 128), F32),
        vec((NBLK, 4, 128), F32),
        vec((NBLK, 4, 128), F32),
        vec((NBLK, 4, 128), F32),
        vec((NBLK, 1, 128), F32),
        vec((3, NSEG, 128), F32),
        vec((NSEG, 128), F32),
        vec((NSEG, PIECES * WIDE), F32),
        vec((ROWS, PIECES * WIDE), F32),
        vec((3, 3, CX + 1) + slab, F32),
        vec((6, CX + 2) + slab, F32),
        vec((3, CX + 1) + slab, F32),
        vec((2, 3, CX + 1, ZT, 32, 128), F32),
        vec((3, ZT, CX, 128), F32),
        vec((3, ZT, CX, 128), F32),
        vec((16, 128), F32),
        vec((16, 128), F32),
        vec((ZT, CX, 128), F32),
        vec((3, CX + 1, ZT, 32, 128), F32),
        vec((3,) + slab, F32),
        vec((3, ZT, CX, 128), F32),
        vec((3, ZT, CX, 128), F32),
        vec((16, 128), F32),
        vec((16, 128), F32),
        vec((3, 8, 128), F32),
        vec((2, 8, 128), F32),
        pltpu.SMEM((TABLE,), I32),
        pltpu.SMEM((NBIN - 1, TABLE), I32),
        dma((5 * ZT,)),
        dma((6,)),
        dma((6,)),
        dma((NBIN - 1,)),
        dma((2, NBIN - 1)),
        dma((1,)),
        dma((1,)),
        dma((2,)),
        dma((2,)),
        dma((NBIN - 1,)),
        dma((NBIN - 1,)),
    ]
    results = pl.pallas_call(
        kernel,
        out_shape=(
            pltpu.VMEM((3, CX) + slab, F32),
            pltpu.VMEM((3, CX) + slab, F32),
            pltpu.VMEM((2, 128), F32),
        ),
        in_specs=[hbm] * 5 + [vmem, vmem, smem],
        out_specs=(vmem, vmem, vmem),
        scratch_shapes=scratch,
        compiler_params=pltpu.CompilerParams(
            collective_id=0, has_side_effects=True, vmem_limit_bytes=65339392
        ),
        name="module_substeps",
    )(
        displacement, velocity, moduli, nodal_mass, element_tile,
        node.reshape(NBLK, SEG), base, contact_bin.transpose(0, 2, 1),
    )
    new_displacement, new_velocity, heat = pl.pallas_call(
        deliver,
        out_shape=(
            jax.ShapeDtypeStruct(displacement.shape, F32),
            jax.ShapeDtypeStruct(velocity.shape, F32),
            jax.ShapeDtypeStruct((2, 128), F32),
        ),
        in_specs=[vmem] * 3,
        out_specs=(hbm, hbm, hbm),
        scratch_shapes=[dma((2 * ZT + 1,))],
        name="deliver",
    )(*[pltpu.with_memory_space_constraint(x, pltpu.VMEM) for x in results])
    return new_displacement, new_velocity, heat.reshape(-1)


def solution(mesh):
    placed = (
        P(None, "dom", "bin", None),
        P(None, "dom", "bin", None),
        P(None, "dom", "bin", None),
        P("dom", "bin", None),
        P(("dom", "bin")),
        P(None, ("dom", "bin")),
        P(None, ("dom", "bin"), None),
        P("dom", "bin", None),
    )
    return jax.shard_map(
        per_device,
        mesh=mesh,
        in_specs=placed,
        out_specs=(P(None, "dom", "bin", None), P(None, "dom", "bin", None), P(("dom", "bin"))),
        check_vma=False,
    )
```

```python
import functools

import jax
import jax.numpy as jnp
from jax import lax
from jax.experimental import pallas as pl
from jax.experimental.pallas import tpu as pltpu
from jax.sharding import PartitionSpec as P

SUB = 4
SEG = 128
TILE_DEV = 256
RADIUS = 0.09
PENALTY = 4.0
SHORT_GAIN = 100.0
TIME_STEP = 0.2

CX, CY, ZT = 8, 16, 4
NBLK, CAP, NBIN = 8, 4, 4
NSEG = NBLK * SEG
ROWS = CX * ZT * CY
PIECES = 2
ROWS_OWN, ROWS_OVER, ROWS_NEXT = 64, 64, 64
WIDE = 384
FAR = 1e12
BINS = SUB * NBIN * CAP
RANKS = BINS + SUB * NBLK
TABLE = RANKS + SUB * NBLK
NEXT, OVER, LAST = NBLK + 1, 2 * (NBLK + 1), 3 * (NBLK + 1)
MESH = pl.DeviceIdType.MESH
F32, BF16, I32 = jnp.float32, jnp.bfloat16, jnp.int32


def pieces_of(value):
    parts = []
    for _ in range(PIECES):
        part = value.astype(BF16)
        parts.append(part)
        value = value - part.astype(F32)
    return parts


def lanes_of(shape):
    return lax.broadcasted_iota(I32, shape, len(shape) - 1)


def next_z(value):
    turned = pltpu.roll(value, 127, 2)
    beyond = jnp.concatenate([turned[1:], turned[:1]], axis=0)
    return jnp.where(lanes_of(value.shape) == 127, beyond, turned)


def last_z(value):
    turned = pltpu.roll(value, 1, 2)
    before = jnp.concatenate([turned[-1:], turned[:-1]], axis=0)
    return jnp.where(lanes_of(value.shape) == 0, before, turned)


def spread_row(row):
    return jnp.broadcast_to(row, (SEG, SEG)).T


def kernel(
    disp_in, velo_in, moduli_in, mass_in, tile_in, node_ref, base_ref, bins_ref,
    disp_out, velo, heat_out,
    disp, moduli, inverse, tiles,
    one_seg, one_node, lane_col, base_col, tile_lane, tile_row, tile_col,
    split_disp, split_push, seg_col, seg_row, pool, spread,
    met_own, met_over, own_rows, return_out, return_in, heat_row,
    push_acc, heat_acc, picked, pushed,
    grads, stress, near, far,
    col_out, col_in, corner_out, corner_in,
    edge, turned, layer_force_in, col_force_out, col_force_in,
    corner_force_out, corner_force_in,
    heat_parts, heat_in, table, tables,
    in_sem, send_sem, recv_sem, point_send, point_recv, return_send, return_recv,
    heat_send, heat_recv, table_send, table_recv,
):
    dom, own = lax.axis_index("dom"), lax.axis_index("bin")
    doms, bins = lax.axis_size("dom"), lax.axis_size("bin")
    dom_up, dom_low = dom < doms - 1, dom > 0
    bin_up, bin_low = own < bins - 1, own > 0
    diag_up, diag_low = jnp.logical_and(dom_up, bin_up), jnp.logical_and(dom_low, bin_low)

    loads = []
    for z in range(ZT):
        z_at = pl.ds(z * 128, 128)
        loads.append((disp_in.at[:, :, :, z_at], disp.at[:, pl.ds(0, CX), z, pl.ds(8, CY), :]))
        loads.append((tile_in.at[:, :, z_at], tiles.at[:, z]))
        loads.append((moduli_in.at[:, :, :, z_at], moduli.at[:, :, z]))
        loads.append((mass_in.at[:, :, z_at], inverse.at[:, z]))
        loads.append((velo_in.at[:, :, :, z_at], velo.at[:, :, z]))
    loads = [pltpu.make_async_copy(a, b, in_sem.at[i]) for i, (a, b) in enumerate(loads)]
    for load in loads:
        load.start()

    disp[:, CX, :, :, :] = jnp.zeros((3, ZT, 32, 128), F32)
    col_in[...] = jnp.zeros_like(col_in)
    corner_in[...] = jnp.zeros_like(corner_in)
    layer_force_in[...] = jnp.zeros_like(layer_force_in)
    col_force_in[...] = jnp.zeros_like(col_force_in)
    corner_force_in[...] = jnp.zeros_like(corner_force_in)
    heat_in[...] = jnp.zeros_like(heat_in)
    for k in range(6):
        stress[k, 0] = jnp.zeros((ZT, CY, 128), F32)
        stress[k, CX + 1] = jnp.zeros((ZT, CY, 128), F32)
    for p in range(3):
        for k in range(2):
            for x in range(CX + 1):
                far[k, p, x, :, 0:8, :] = jnp.zeros((ZT, 8, 128), F32)
        for i in range(NBIN):
            spread[i * (NBLK + 1) + NBLK, p] = jnp.full((8, 128), FAR, F32)
    met_own[NBLK] = jnp.zeros((2, 4, 8, 128), F32)
    met_over[NBLK] = jnp.zeros((2, 4, 8, 128), F32)
    heat_row[...] = jnp.zeros_like(heat_row)

    barrier = pltpu.get_barrier_semaphore()
    peers = [(dom, lax.rem(own + i, bins), None) for i in range(1, NBIN)]
    peers += [(dom + 1, own, dom_up), (dom - 1, own, dom_low)]
    peers += [(dom + 1, own + 1, diag_up), (dom - 1, own - 1, diag_low)]
    for to_dom, to_bin, exists in peers:
        def greet(to_dom=to_dom, to_bin=to_bin):
            pl.semaphore_signal(barrier, inc=1, device_id=(to_dom, to_bin), device_id_type=MESH)
        if exists is None:
            greet()
        else:
            pl.when(exists)(greet)

    def fill_slots(step, carry):
        named = [bins_ref[step, 0, b] for b in range(NBLK)]
        for b in range(NBLK):
            rank = jnp.int32(0)
            for before in range(b):
                rank = rank + (named[before] == named[b]).astype(I32)
            table[RANKS + step * NBLK + b] = rank & (CAP - 1)
            table[BINS + step * NBLK + b] = named[b]
        for k in range(NBIN):
            count = jnp.int32(0)
            found = [jnp.int32(NBLK)] * CAP
            for b in range(NBLK):
                same = named[b] == k
                for rank in range(CAP):
                    found[rank] = jnp.where(
                        jnp.logical_and(same, count == rank), jnp.int32(b), found[rank]
                    )
                count = count + same.astype(I32)
            for rank in range(CAP):
                table[(step * NBIN + k) * CAP + rank] = found[rank]
        return carry

    lax.fori_loop(0, SUB, fill_slots, 0)

    eye = lax.broadcasted_iota(I32, (SEG, SEG), 0) == lanes_of((SEG, SEG))

    def place_block(b):
        node = node_ref[pl.ds(b, 1), :]
        x, y = lax.shift_right_logical(node, 13), lax.shift_right_logical(node, 9) & 15
        z = lax.shift_right_logical(node, 7) & 3
        row = (x * ZT + z) * CY + y
        lane = node & 127
        at = pl.ds(pl.multiple_of(b * SEG, SEG), SEG)
        row_ids = lax.broadcasted_iota(I32, (ROWS, SEG), 0)
        one_seg[:, at] = jnp.where(row_ids == row, 1.0, 0.0).astype(BF16)
        row_col = spread_row(row.astype(F32))
        ids = lanes_of((SEG, SEG)).astype(F32)
        for part in range(ROWS // 128):
            hits = jnp.where(row_col == ids + float(128 * part), 1.0, 0.0).astype(BF16)
            one_node[at, part * 128 : part * 128 + 128] = hits
        lane_col[at, :] = spread_row(lane.astype(F32))
        for c in range(3):
            base_col[c, at, :] = spread_row(base_ref[c : c + 1, at])
        heat_acc[at, :] = jnp.zeros((SEG, SEG), F32)

    def place_pair(pair, carry):
        for b in (2 * pair, 2 * pair + 1):
            place_block(b)
        return carry

    lax.fori_loop(0, NBLK // 2, place_pair, 0)

    for load in loads:
        load.wait()

    def scale(x, carry):
        for k in range(2):
            moduli[k, x] = moduli[k, x] * -0.0625
        inverse[x] = TIME_STEP / inverse[x]
        return carry

    lax.fori_loop(0, CX, scale, 0)

    greeted = jnp.int32(NBIN - 1)
    for _, _, exists in peers[NBIN - 1 :]:
        greeted = greeted + exists.astype(I32)
    pl.semaphore_wait(barrier, greeted)

    def remote(src, dst, index, to_dom, to_bin):
        return pltpu.make_async_remote_copy(
            src_ref=src, dst_ref=dst, send_sem=send_sem.at[index], recv_sem=recv_sem.at[index],
            device_id=(to_dom, to_bin), device_id_type=MESH,
        )

    def table_copy(i):
        return pltpu.make_async_remote_copy(
            src_ref=table, dst_ref=tables.at[i],
            send_sem=table_send.at[i], recv_sem=table_recv.at[i],
            device_id=(dom, lax.rem(own + bins - 1 - i, bins)), device_id_type=MESH,
        )

    for i in range(NBIN - 1):
        table_copy(i).start()
    inner = pl.ds(8, CY)
    layer_copy = remote(disp.at[:, 0, :, inner, :], disp.at[:, CX, :, inner, :], 0, dom - 1, own)
    col_copy = remote(col_out, col_in, 1, dom, own - 1)
    corner_copy = remote(corner_out, corner_in, 2, dom - 1, own - 1)
    layer_force_copy = remote(near.at[:, CX], layer_force_in, 3, dom + 1, own)
    col_force_copy = remote(col_force_out, col_force_in, 4, dom, own + 1)
    corner_force_copy = remote(corner_force_out, corner_force_in, 5, dom + 1, own + 1)

    def touching(step, slots_of, met, rows, alone):
        def with_block(b, carry):
            facing = slots_of(step, *mine_of(table, step, b))

            def with_rows(g, met_sums):
                met_sums = [list(each) for each in met_sums]
                at = pl.ds(pl.multiple_of(b * SEG + g * rows, rows), rows)
                wide = (rows // 8, 8, 128)
                mine = [seg_col[c, at, :].reshape(wide) for c in range(3)]
                if met is met_own:
                    sums = [jnp.zeros(wide, F32) for c in range(3)]
                else:
                    sums = [push_acc[c, at, :].reshape(wide) for c in range(3)]
                heat = heat_acc[at, :].reshape(wide)
                for j, slot in enumerate(facing):
                    delta = [mine[c] - spread[slot, c] for c in range(3)]
                    square = delta[0] * delta[0] + delta[1] * delta[1] + delta[2] * delta[2]
                    square = jnp.maximum(square, 1e-30)
                    over = lax.rsqrt(square)
                    pressure = jnp.maximum(RADIUS - square * over, 0.0)
                    weight = pressure * jnp.minimum(over, 1.0 / (0.25 * RADIUS))
                    parts = [weight * delta[c] for c in range(3)] + [pressure * pressure]
                    sums = [sums[c] + parts[c] for c in range(3)]
                    heat = heat + parts[3]
                    if j < alone:
                        continue
                    row = met_sums[j - alone]
                    for q in range(4):
                        row[q] = row[q] + jnp.sum(parts[q], axis=0)
                for c in range(3):
                    push_acc[c, at, :] = sums[c].reshape(rows, 128)
                heat_acc[at, :] = heat.reshape(rows, 128)
                return met_sums

            none = [[jnp.zeros((8, 128), F32)] * 4 for _ in facing[alone:]]
            met_sums = lax.fori_loop(0, SEG // rows, with_rows, none)
            for j, each in enumerate(met_sums):
                for q in range(4):
                    met[b, j, q] = each[q]
            return carry

        lax.fori_loop(0, NBLK, with_block, 0)

    high = (own >= NBIN // 2).astype(I32)

    def mine_of(numbers, step, b):
        return numbers[BINS + step * NBLK + b], numbers[RANKS + step * NBLK + b]

    def own_slots(step, named, rank):
        base = step * (NBIN * CAP) + named * CAP
        opposite = table[base + ((rank + 2) & (CAP - 1))]
        opposite = jnp.where(rank < CAP // 2, opposite, NBLK)
        return [table[base + rank], table[base + ((rank + 1) & (CAP - 1))], opposite]

    def next_slots(step, named, rank):
        base = step * (NBIN * CAP) + named * CAP
        ahead = [NEXT + tables[0, base + k] for k in range(CAP)]
        return ahead + [LAST + tables[2, base + k] for k in range(CAP)]

    def over_slots(step, named, rank):
        first = step * (NBIN * CAP) + named * CAP + ((rank + high) & 1)
        return [OVER + tables[1, first], OVER + tables[1, first + 2]]

    def rows_of(values):
        return jnp.sum(functools.reduce(lambda a, b: a + b, values), axis=0, keepdims=True)

    device = dom * bins + own

    def find_tiles():

        def split_tiles(x, carry):
            offset = tiles[x] - device * TILE_DEV + bins * TILE_DEV
            side = lax.shift_right_logical(offset, 10)
            row = side * 2 + (lax.shift_right_logical(offset, 7) & 1)
            at = pl.ds(pl.multiple_of(x * (ZT * CY), ZT * CY), ZT * CY)
            split_disp[0, at, :] = row.astype(F32).astype(BF16).reshape(ZT * CY, 128)
            lane = (offset & 127).astype(F32).astype(BF16)
            split_disp[1, at, :] = lane.reshape(ZT * CY, 128)
            return carry

        lax.fori_loop(0, CX, split_tiles, 0)
        side_by_side = jnp.concatenate([split_disp[0], split_disp[1]], axis=1)
        picked[:, 0:256] = jnp.dot(one_node[...], side_by_side, preferred_element_type=F32)

        def place_tiles(b, carry):
            at = pl.ds(pl.multiple_of(b * SEG, SEG), SEG)
            ids = lanes_of((SEG, SEG)).astype(F32)
            mask = lane_col[at, :] == ids
            row_col = jnp.sum(jnp.where(mask, picked[at, 0:128], 0.0), axis=1, keepdims=True)
            lane = jnp.sum(jnp.where(mask, picked[at, 128:256], 0.0), axis=1, keepdims=True)
            tile_col[at, :] = jnp.broadcast_to(lane, (SEG, SEG))
            row = jnp.sum(jnp.where(eye, row_col, 0.0), axis=0, keepdims=True)
            ids = lax.broadcasted_iota(I32, (16, SEG), 0).astype(F32)
            tile_row[:, at] = jnp.where(ids == row, 1.0, 0.0).astype(BF16)
            return carry

        lax.fori_loop(0, NBLK, place_tiles, 0)

    def heat_copy(index, to_dom):
        return pltpu.make_async_remote_copy(
            src_ref=heat_parts.at[2 * index], dst_ref=heat_in.at[index],
            send_sem=heat_send.at[index], recv_sem=heat_recv.at[index],
            device_id=(to_dom, own), device_id_type=MESH,
        )

    to_low, to_up = heat_copy(0, dom - 1), heat_copy(1, dom + 1)

    def send_heat():
        def lay_heat(b, carry):
            at = pl.ds(pl.multiple_of(b * SEG, SEG), SEG)
            met = heat_row[b] + own_rows[b, 3:4, :] + return_in[b, 3:4, :]
            total = heat_acc[at, :] + jnp.where(eye, met, 0.0)
            total = SHORT_GAIN * jnp.sum(total, axis=1, keepdims=True)
            laid = jnp.where(tile_col[at, :] == lanes_of((SEG, SEG)).astype(F32), total, 0.0)
            for p, part in enumerate(pieces_of(laid)):
                tile_lane[at, p * 128 : p * 128 + 128] = part
            return carry

        lax.fori_loop(0, NBLK, lay_heat, 0)
        laid = jnp.dot(tile_row[...], tile_lane[...], preferred_element_type=F32)
        on_tiles = laid[:, 0:128] + laid[:, 128:256]
        for side in range(3):
            heat_parts[side, 0:2, :] = on_tiles[side * 2 : side * 2 + 2, :]
        pl.when(dom_low)(to_low.start)
        pl.when(dom_up)(to_up.start)

    def substep(step, carry):
        parity = lax.rem(step, 2)

        for c in range(3):
            for z in range(ZT):
                corner_out[c * ZT + z : c * ZT + z + 1, :] = disp[c, 0, z, 8:9, :]
                for x in range(CX):
                    col_out[c, z, x : x + 1, :] = disp[c, x, z, 8:9, :]
        pl.when(bin_low)(col_copy.start)
        pl.when(diag_low)(corner_copy.start)

        def split(pair, carry):
            for x in (2 * pair, 2 * pair + 1):
                at = pl.ds(pl.multiple_of(x * (ZT * CY), ZT * CY), ZT * CY)
                for c in range(3):
                    value = disp[c, x, :, 8 : 8 + CY, :].reshape(ZT * CY, 128)
                    for p, part in enumerate(pieces_of(value)):
                        split_disp[p * 3 + c, at, :] = part
            return carry

        lax.fori_loop(0, CX // 2, split, 0)
        side_by_side = jnp.concatenate([split_disp[k] for k in range(PIECES * 3)], axis=1)
        picked[...] = jnp.dot(one_node[...], side_by_side, preferred_element_type=F32)

        def positions(pair, carry):
            for b in (2 * pair, 2 * pair + 1):
                at = pl.ds(pl.multiple_of(b * SEG, SEG), SEG)
                mask = lane_col[at, :] == lanes_of((SEG, SEG)).astype(F32)
                for c in range(3):
                    parts = [
                        jnp.where(mask, picked[at, k : k + 128], 0.0)
                        for k in range(c * 128, PIECES * WIDE, WIDE)
                    ]
                    total = jnp.sum(parts[0] + parts[1], axis=1, keepdims=True)
                    column = base_col[c, at, :] + total
                    seg_col[c, at, :] = column
                    row = jnp.sum(jnp.where(eye, column, 0.0), axis=0, keepdims=True)
                    seg_row[c, pl.ds(b, 1), :] = row
                    spread[b, c] = jnp.broadcast_to(row, (8, 128))
            return carry

        lax.fori_loop(0, NBLK // 2, positions, 0)
        for i in (1, 0, 2):
            point_copy(i, parity).start()

        touching(step, own_slots, met_own, ROWS_OWN, 1)

        def gather_own(b, carry):
            named, rank = mine_of(table, step, b)
            base = step * (NBIN * CAP) + named * CAP
            beside = table[base + ((rank + 3) & (CAP - 1))]
            opposite = table[base + ((rank + 2) & (CAP - 1))]
            opposite = jnp.where(rank >= CAP // 2, opposite, NBLK)
            for q in range(4):
                row = rows_of([met_own[beside, 0, q], met_own[opposite, 1, q]])
                own_rows[b, q : q + 1, :] = row
            return carry

        lax.fori_loop(0, NBLK, gather_own, 0)

        pl.when(bin_up)(col_copy.wait_recv)
        for c in range(3):
            for z in range(ZT):
                for x in range(CX):
                    disp[c, x, z, 24:25, :] = col_in[c, z, x : x + 1, :]
            edge[...] = next_z(col_in[c])
            for z in range(ZT):
                for x in range(CX):
                    turned[c, x, z, 24:25, :] = edge[z, x : x + 1, :]

        def corners_on(x):
            for c in range(3):
                low, high = disp[c, x, :, 8:24, :], disp[c, x, :, 9:25, :]
                low_next = next_z(low)
                turned[c, x, :, 8:24, :] = low_next
                high_next = turned[c, x, :, 9:25, :]
                at_low, at_high = low + low_next, high + high_next
                grads[c, 0, x] = at_low + at_high
                grads[c, 1, x] = at_high - at_low
                grads[c, 2, x] = (low_next - low) + (high_next - high)

        def corners(part, carry):
            for x in [4 * part + i for i in range(4)]:
                corners_on(x)
            return carry

        lax.fori_loop(0, CX // 4, corners, 0)

        def stresses_on(x):
            g = [
                [grads[c, 0, x + 1] - grads[c, 0, x]]
                + [grads[c, q, x] + grads[c, q, x + 1] for q in (1, 2)]
                for c in range(3)
            ]
            lame, shear = moduli[0, x], moduli[1, x]
            volume = lame * (g[0][0] + g[1][1] + g[2][2])
            for p in range(3):
                stress[p, x + 1] = shear * (g[p][p] + g[p][p]) + volume
            stress[3, x + 1] = shear * (g[0][1] + g[1][0])
            stress[4, x + 1] = shear * (g[0][2] + g[2][0])
            stress[5, x + 1] = shear * (g[1][2] + g[2][1])

        def stresses(x, carry):
            stresses_on(x)
            return carry

        lax.fori_loop(0, CX - 1, stresses, 0)
        pl.when(dom_up)(layer_copy.wait_recv)
        pl.when(diag_up)(corner_copy.wait_recv)
        for c in range(3):
            for z in range(ZT):
                disp[c, CX, z, 24:25, :] = corner_in[c * ZT + z : c * ZT + z + 1, :]
            turned[c, CX, :, 24:32, :] = next_z(disp[c, CX, :, 24:32, :])
        corners_on(CX)
        stresses_on(CX - 1)

        def forces_on(x):
            for p, (kx, ky, kz) in enumerate(((0, 3, 4), (3, 1, 5), (4, 5, 2))):
                along_x = stress[kx, x] - stress[kx, x + 1]
                along_y = stress[ky, x] + stress[ky, x + 1]
                along_z = stress[kz, x] + stress[kz, x + 1]
                minus, plus = along_x - along_y, along_x + along_y
                far[0, p, x, :, 8:24, :] = plus - along_z
                far[1, p, x, :, 8:24, :] = plus + along_z
                here = minus - along_z + far[0, p, x, :, 7:23, :]
                near[p, x] = here + last_z(minus + along_z + far[1, p, x, :, 7:23, :])

        forces_on(CX)
        for p in range(3):
            ends = far[0, p, CX, :, 16:24, :] + last_z(far[1, p, CX, :, 16:24, :])
            for z in range(ZT):
                corner_force_out[p * ZT + z : p * ZT + z + 1, :] = ends[z, 7:8, :]
        pl.when(dom_up)(layer_force_copy.start)
        pl.when(diag_up)(corner_force_copy.start)

        def forces(pair, carry):
            for x in (2 * pair, 2 * pair + 1):
                forces_on(x)
            return carry

        lax.fori_loop(0, CX // 2, forces, 0)
        for p in range(3):
            for z in range(ZT):
                for x in range(CX):
                    col_force_out[p, z, x : x + 1, :] = far[0, p, x, z, 23:24, :]
                    edge[z, x : x + 1, :] = far[1, p, x, z, 23:24, :]
            col_force_out[p] = col_force_out[p] + last_z(edge[...])
        pl.when(bin_up)(col_force_copy.start)

        pl.when(step == 1)(find_tiles)

        @pl.when(step == 0)
        def tables_here():
            for i in range(NBIN - 1):
                table_copy(i).wait()

        def spread_from(i):
            point_copy(i, parity).wait_recv()
            for b in range(NBLK):
                for c in range(3):
                    spread[NEXT * (i + 1) + b, c] = jnp.broadcast_to(
                        pool[parity, i, c, b : b + 1, :], (8, 128)
                    )

        spread_from(1)
        touching(step, over_slots, met_over, ROWS_OVER, 0)

        def gather_over(b, carry):
            named, rank = mine_of(tables.at[1], step, b)
            first = step * (NBIN * CAP) + named * CAP + ((rank + high) & 1)
            ones = [table[first], table[first + 2]]
            half = lax.shift_right_logical(rank, 1)
            for q in range(4):
                row = rows_of([met_over[one, half, q] for one in ones])
                return_out[b, q : q + 1, :] = row
            return carry

        lax.fori_loop(0, NBLK, gather_over, 0)
        return_copy.start()
        spread_from(0)
        spread_from(2)
        touching(step, next_slots, None, ROWS_NEXT, 2 * CAP)

        return_copy.wait_recv()
        pl.when(step == SUB - 1)(send_heat)


        def lay_push(pair, carry):
            for b in (2 * pair, 2 * pair + 1):
                at = pl.ds(pl.multiple_of(b * SEG, SEG), SEG)
                mask = lane_col[at, :] == lanes_of((SEG, SEG)).astype(F32)
                met = own_rows[b] + return_in[b]
                heat_row[b] = heat_row[b] + met[3:4, :]
                for c in range(3):
                    total = push_acc[c, at, :] - jnp.where(eye, met[c : c + 1, :], 0.0)
                    total = jnp.sum(total, axis=1, keepdims=True)
                    laid = jnp.where(mask, PENALTY * total, 0.0)
                    for p, part in enumerate(pieces_of(laid)):
                        split_push[p * 3 + c, at, :] = part
            return carry

        lax.fori_loop(0, NBLK // 2, lay_push, 0)
        side_by_side = jnp.concatenate([split_push[k] for k in range(PIECES * 3)], axis=1)
        pushed[...] = jnp.dot(one_seg[...], side_by_side, preferred_element_type=F32)

        pl.when(dom_low)(layer_force_copy.wait_recv)
        pl.when(bin_low)(col_force_copy.wait_recv)
        pl.when(diag_low)(corner_force_copy.wait_recv)
        for p in range(3):
            near[p, 0] = near[p, 0] + layer_force_in[p]
            for z in range(ZT):
                near[p, 0, z, 0:1, :] = (
                    near[p, 0, z, 0:1, :] + corner_force_in[p * ZT + z : p * ZT + z + 1, :]
                )
                for x in range(CX):
                    near[p, x, z, 0:1, :] = (
                        near[p, x, z, 0:1, :] + col_force_in[p, z, x : x + 1, :]
                    )
        pl.when(dom_low)(layer_copy.wait_send)
        pl.when(bin_low)(col_copy.wait_send)
        pl.when(diag_low)(corner_copy.wait_send)
        pl.when(dom_up)(layer_force_copy.wait_send)
        pl.when(bin_up)(col_force_copy.wait_send)
        pl.when(diag_up)(corner_force_copy.wait_send)
        for i in range(NBIN - 1):
            point_copy(i, parity).wait_send()
        return_copy.wait_send()

        def advance_on(x):
            at = pl.ds(x * (ZT * CY), ZT * CY)
            for p in range(3):
                force = near[p, x]
                for part in range(PIECES):
                    column = part * WIDE + p * 128
                    force = force + pushed[at, column : column + 128].reshape(ZT, CY, 128)
                moved = velo[p, x] + force * inverse[x]
                velo[p, x] = moved
                moved = disp[p, x, :, 8:24, :] + TIME_STEP * moved
                disp[p, x, :, 8:24, :] = moved
                disp_out[p, x] = moved

        def advance(x, carry):
            advance_on(pl.multiple_of(x, 1))
            return carry

        advance_on(0)
        pl.when(jnp.logical_and(dom_low, step < SUB - 1))(layer_copy.start)
        lax.fori_loop(1, CX, advance, 0)
        return carry

    def point_copy(i, parity):
        return pltpu.make_async_remote_copy(
            src_ref=seg_row, dst_ref=pool.at[parity, i],
            send_sem=point_send.at[i], recv_sem=point_recv.at[parity, i],
            device_id=(dom, lax.rem(own + bins - 1 - i, bins)), device_id_type=MESH,
        )

    return_copy = pltpu.make_async_remote_copy(
        src_ref=return_out, dst_ref=return_in, send_sem=return_send.at[0],
        recv_sem=return_recv.at[0], device_id=(dom, lax.rem(own + 2, bins)), device_id_type=MESH,
    )

    pl.when(dom_low)(layer_copy.start)
    lax.fori_loop(0, SUB, substep, 0)

    pl.when(dom_up)(to_low.wait_recv)
    pl.when(dom_low)(to_up.wait_recv)
    heat_out[...] = heat_parts[1, 0:2, :] + heat_in[0, 0:2, :] + heat_in[1, 0:2, :]
    pl.when(dom_low)(to_low.wait_send)
    pl.when(dom_up)(to_up.wait_send)


def deliver(disp, velo, heat, disp_out, velo_out, heat_out, sem):
    stores = [(heat, heat_out)]
    for z in range(ZT):
        z_at = pl.ds(z * 128, 128)
        stores.append((disp.at[:, :, z], disp_out.at[:, :, :, z_at]))
        stores.append((velo.at[:, :, z], velo_out.at[:, :, :, z_at]))
    stores = [pltpu.make_async_copy(a, b, sem.at[i]) for i, (a, b) in enumerate(stores)]
    for store in stores:
        store.start()
    for store in stores:
        store.wait()


def per_device(displacement, velocity, moduli, nodal_mass, node, base, contact_bin, element_tile):
    anywhere = pl.BlockSpec(memory_space=pl.ANY)
    hbm = pl.BlockSpec(memory_space=pltpu.HBM)
    vmem = pl.BlockSpec(memory_space=pltpu.VMEM)
    smem = pl.BlockSpec(memory_space=pltpu.SMEM)
    dma, vec = pltpu.SemaphoreType.DMA, pltpu.VMEM
    slab = (ZT, CY, 128)
    scratch = [
        vec((3, CX + 1, ZT, 32, 128), F32),
        vec((2, CX) + slab, F32),
        vec((CX,) + slab, F32),
        vec((CX,) + slab, I32),
        vec((ROWS, NSEG), BF16),
        vec((NSEG, ROWS), BF16),
        vec((NSEG, 128), F32),
        vec((3, NSEG, 128), F32),
        vec((NSEG, PIECES * 128), BF16),
        vec((16, NSEG), BF16),
        vec((NSEG, 128), F32),
        vec((PIECES * 3, ROWS, 128), BF16),
        vec((PIECES * 3, NSEG, 128), BF16),
        vec((3, NSEG, 128), F32),
        vec((3, NBLK, 128), F32),
        vec((2, NBIN - 1, 3, NBLK, 128), F32),
        vec((NBIN * (NBLK + 1), 3, 8, 128), F32),
        vec((NBLK + 1, 2, 4, 8, 128), F32),
        vec((NBLK + 1, 2, 4, 8, 128), F32),
        vec((NBLK, 4, 128), F32),
        vec((NBLK, 4, 128), F32),
        vec((NBLK, 4, 128), F32),
        vec((NBLK, 1, 128), F32),
        vec((3, NSEG, 128), F32),
        vec((NSEG, 128), F32),
        vec((NSEG, PIECES * WIDE), F32),
        vec((ROWS, PIECES * WIDE), F32),
        vec((3, 3, CX + 1) + slab, F32),
        vec((6, CX + 2) + slab, F32),
        vec((3, CX + 1) + slab, F32),
        vec((2, 3, CX + 1, ZT, 32, 128), F32),
        vec((3, ZT, CX, 128), F32),
        vec((3, ZT, CX, 128), F32),
        vec((16, 128), F32),
        vec((16, 128), F32),
        vec((ZT, CX, 128), F32),
        vec((3, CX + 1, ZT, 32, 128), F32),
        vec((3,) + slab, F32),
        vec((3, ZT, CX, 128), F32),
        vec((3, ZT, CX, 128), F32),
        vec((16, 128), F32),
        vec((16, 128), F32),
        vec((3, 8, 128), F32),
        vec((2, 8, 128), F32),
        pltpu.SMEM((TABLE,), I32),
        pltpu.SMEM((NBIN - 1, TABLE), I32),
        dma((5 * ZT,)),
        dma((6,)),
        dma((6,)),
        dma((NBIN - 1,)),
        dma((2, NBIN - 1)),
        dma((1,)),
        dma((1,)),
        dma((2,)),
        dma((2,)),
        dma((NBIN - 1,)),
        dma((NBIN - 1,)),
    ]
    results = pl.pallas_call(
        kernel,
        out_shape=(
            pltpu.VMEM((3, CX) + slab, F32),
            pltpu.VMEM((3, CX) + slab, F32),
            pltpu.VMEM((2, 128), F32),
        ),
        in_specs=[hbm] * 5 + [vmem, vmem, smem],
        out_specs=(vmem, vmem, vmem),
        scratch_shapes=scratch,
        compiler_params=pltpu.CompilerParams(
            collective_id=0, has_side_effects=True, vmem_limit_bytes=65339392
        ),
        name="module_substeps",
    )(
        displacement, velocity, moduli, nodal_mass, element_tile,
        node.reshape(NBLK, SEG), base, contact_bin.transpose(0, 2, 1),
    )
    new_displacement, new_velocity, heat = pl.pallas_call(
        deliver,
        out_shape=(
            jax.ShapeDtypeStruct(displacement.shape, F32),
            jax.ShapeDtypeStruct(velocity.shape, F32),
            jax.ShapeDtypeStruct((2, 128), F32),
        ),
        in_specs=[vmem] * 3,
        out_specs=(hbm, hbm, hbm),
        scratch_shapes=[dma((2 * ZT + 1,))],
        name="deliver",
    )(*[pltpu.with_memory_space_constraint(x, pltpu.VMEM) for x in results])
    return new_displacement, new_velocity, heat.reshape(-1)


def solution(mesh):
    placed = (
        P(None, "dom", "bin", None),
        P(None, "dom", "bin", None),
        P(None, "dom", "bin", None),
        P("dom", "bin", None),
        P(("dom", "bin")),
        P(None, ("dom", "bin")),
        P(None, ("dom", "bin"), None),
        P("dom", "bin", None),
    )
    return jax.shard_map(
        per_device,
        mesh=mesh,
        in_specs=placed,
        out_specs=(P(None, "dom", "bin", None), P(None, "dom", "bin", None), P(("dom", "bin"))),
        check_vma=False,
    )
```
